32 devices in a mesh: section: 4 (over y, x), row: 2 (over core), col: 4 (over z).
Axes of the slice: x: 2, y: 2, z: 4, core: 2. Of those that a mesh axis runs over, the one named last changes fastest.
Arguments:
- latent: bfloat16 [16, 8, 64, 256], P('section', 'row', 'col'), may hold values from -6 to 6
- w_first: bfloat16 [3, 3, 3, 256, 256], replicated, may hold values from -0.078125 to 0.078125
- w_second: bfloat16 [3, 3, 3, 256, 128], replicated, may hold values from -0.078125 to 0.078125
- w_third: bfloat16 [3, 3, 3, 128, 128], replicated, may hold values from -0.109375 to 0.109375
Outputs:
- decoded: bfloat16 [16, 16, 128, 128], P('section', 'row', 'col')
The draws below stay inside these ranges and needn't reach their ends.
All inputs are finite; a program needn't handle non-finite values.
Results may differ from the reference program's by a relative error of at most 0.0057.
Values may be sent and summed in bfloat16 or wider, within the bound.
No kernel may reach another device: no remote copies, remote signals or barrier semaphores. Data moves between devices by JAX's collectives and lax.ppermute only.
A program may use at most 64 MiB of HBM per device.

```python
import jax
import jax.numpy as jnp
from jax import lax

LAT_CH = 256
MID_CH = 128
FRAMES = 16
H = 8
W = 64


def levels(key, extent, pieces, low, largest):
    def one(dim, parts):
        draws = jax.random.uniform(jax.random.fold_in(jax.random.fold_in(key, 6), dim), (parts,), jnp.float32, low / len(pieces), largest / len(pieces))
        return jnp.repeat(jnp.exp(draws), extent[dim] // parts).reshape((-1,) + (1,) * (len(extent) - dim - 1))

    gain = one(*pieces[0])
    for cut in pieces[1:]:
        gain = gain * one(*cut)
    return gain


def bell_draw(own_key, dims, scale, limit, cuts=(), kind=jnp.bfloat16):
    values = jax.random.normal(own_key, dims, jnp.float32) * scale
    if len(cuts) > 0:
        values = levels(own_key, dims, cuts, -0.22, 0.18) * values
    return jnp.clip(values, min=-limit, max=limit).astype(kind)


def setup_inputs(seed: int = 0) -> dict:
    keys = jax.random.split(jax.random.key(seed), 5)
    return {
        "latent": bell_draw(keys[0], (FRAMES, H, W, LAT_CH), 1.0, 6.0, ((0, 4), (1, 2), (2, 4))),
        "w_first": bell_draw(keys[1], (3, 3, 3, LAT_CH, LAT_CH), (27 * LAT_CH) ** -0.5, 0.078125),
        "w_second": bell_draw(keys[2], (3, 3, 3, LAT_CH, MID_CH), (27 * LAT_CH) ** -0.5, 0.078125),
        "w_third": bell_draw(keys[3], (3, 3, 3, MID_CH, MID_CH), (27 * MID_CH) ** -0.5, 0.109375),
    }


def causal_conv(field, kernel):
    padded = jnp.pad(field, ((2, 0), (1, 1), (1, 1), (0, 0)))
    result = lax.conv_general_dilated(padded[None], kernel, (1, 1, 1), "VALID", dimension_numbers=("NDHWC", "DHWIO", "NDHWC"), precision=lax.Precision.HIGHEST)
    return result[0]


def upsample(field):
    frames, height, breadth, width = field.shape
    grown = jnp.broadcast_to(field[:, :, None, :, None, :], (frames, height, 2, breadth, 2, width))
    return grown.reshape(frames, 2 * height, 2 * breadth, width)


def reference(latent, w_first, w_second, w_third):
    first = causal_conv(latent.astype(jnp.float32), w_first.astype(jnp.float32)).astype(jnp.bfloat16)
    grown = jnp.maximum(upsample(first), 0)
    second = jnp.maximum(causal_conv(grown.astype(jnp.float32), w_second.astype(jnp.float32)), 0.0).astype(jnp.bfloat16)
    decoded = causal_conv(second.astype(jnp.float32), w_third.astype(jnp.float32))
    return decoded.astype(jnp.bfloat16)
```

```python
import jax
import jax.numpy as jnp
from jax import lax
from jax.sharding import PartitionSpec as P


def ring(x, axis, by):
    size = lax.axis_size(axis)
    return lax.ppermute(x, axis, [(i, (i + by) % size) for i in range(size)])


def earlier_frames(x, count):
    size, length = lax.axis_size("section"), x.shape[0]
    place = lax.axis_index("section")
    pieces, by, left = [], 1, count
    while left > 0:
        take = min(left, length)
        got = ring(x[length - take :], "section", by % size)
        pieces.insert(0, jnp.where(place >= by, got, 0))
        left -= take
        by += 1
    return pieces


def edges(x, axis, dim, width):
    size, length = lax.axis_size(axis), x.shape[dim]
    place = lax.axis_index(axis)
    first = lax.slice_in_dim(x, 0, width, axis=dim)
    last = lax.slice_in_dim(x, length - width, length, axis=dim)
    if size % 2:
        before, after = ring(last, axis, 1), ring(first, axis, size - 1)
    else:
        even = place % 2 == 0
        pairs = [(i, i + 1) for i in range(0, size, 2)]
        swap = pairs + [(j, i) for i, j in pairs]
        got = lax.ppermute(jnp.where(even, last, first), axis, swap)
        if size == 2:
            before = after = got
        else:
            pairs = [(i, (i + 1) % size) for i in range(1, size, 2)]
            swap = pairs + [(j, i) for i, j in pairs]
            other = lax.ppermute(jnp.where(even, first, last), axis, swap)
            before = jnp.where(even, other, got)
            after = jnp.where(even, got, other)
    before = jnp.where(place > 0, before, 0)
    after = jnp.where(place < size - 1, after, 0)
    return before, after


def inside(shape, axis, dim, low, count):
    place = lax.axis_index(axis) * count + low + lax.broadcasted_iota(jnp.int32, shape, dim)
    return (place >= 0) & (place < lax.axis_size(axis) * count)


def conv(x, kernel):
    return lax.conv_general_dilated(
        x[None], kernel, (1, 1, 1), "VALID",
        dimension_numbers=("NDHWC", "DHWIO", "NDHWC"), preferred_element_type=jnp.float32,
    )[0]


def corner_kernel(kernel, dim):
    k = [lax.index_in_dim(kernel, i, dim, keepdims=False) for i in range(3)]
    return [[k[0] + k[1], k[2]], [k[0], k[1] + k[2]]]


def second_kernel(kernel):
    kernel = kernel.astype(jnp.float32)
    rows = corner_kernel(kernel, 1)
    outs = []
    for py in range(2):
        for px in range(2):
            taps = jnp.stack(
                [jnp.stack(corner_kernel(rows[py][di], 1)[px], 1) for di in range(2)], 1
            )
            outs.append(taps)
    return jnp.concatenate(outs, -1).astype(jnp.bfloat16)


def third_kernel(kernel):
    zero = jnp.zeros_like(kernel[:, 0, 0])
    rows = []
    for di in range(2):
        cols = []
        for dj in range(2):
            ins = []
            for py in range(2):
                for px in range(2):
                    outs = []
                    for qy in range(2):
                        for qx in range(2):
                            b, e = 2 * di + py - qy, 2 * dj + px - qx
                            outs.append(kernel[:, b, e] if 0 <= b < 3 and 0 <= e < 3 else zero)
                    ins.append(jnp.concatenate(outs, -1))
            cols.append(jnp.concatenate(ins, -2))
        rows.append(jnp.stack(cols, 1))
    return jnp.stack(rows, 1)


def per_device(latent, w_first, w_second, w_third):
    height, breadth = latent.shape[1:3]
    x = jnp.concatenate([*earlier_frames(latent, 6), latent], 0)
    before, after = edges(x, "row", 1, 2)
    x = jnp.concatenate([before, x, after], 1)
    before, after = edges(x, "col", 2, 2)
    x = jnp.concatenate([before, x, after], 2)
    first = jnp.maximum(conv(x, w_first).astype(jnp.bfloat16), 0)
    keep = inside(first.shape, "row", 1, -1, height) & inside(first.shape, "col", 2, -1, breadth)
    first = jnp.where(keep, first, 0)
    second = jnp.maximum(conv(first, second_kernel(w_second)), 0.0).astype(jnp.bfloat16)
    width = second.shape[-1] // 4
    part = lax.broadcasted_iota(jnp.int32, second.shape, 3) // width
    row = 2 * lax.broadcasted_iota(jnp.int32, second.shape, 1) + part // 2 - 1
    col = 2 * lax.broadcasted_iota(jnp.int32, second.shape, 2) + part % 2 - 1
    row += lax.axis_index("row") * 2 * height
    col += lax.axis_index("col") * 2 * breadth
    keep = (row >= 0) & (row < 2 * height * lax.axis_size("row"))
    keep &= (col >= 0) & (col < 2 * breadth * lax.axis_size("col"))
    second = jnp.where(keep, second, 0)
    out = conv(second, third_kernel(w_third)).astype(jnp.bfloat16)
    frames, width = out.shape[0], w_third.shape[-1]
    out = out.reshape(frames, height, breadth, 2, 2, width).transpose(0, 1, 3, 2, 4, 5)
    return out.reshape(frames, 2 * height, 2 * breadth, width)


def solution(mesh):
    in_specs = (P("section", "row", "col", None), P(), P(), P())
    out_specs = P("section", "row", "col", None)
    return jax.shard_map(
        per_device, mesh=mesh, in_specs=in_specs, out_specs=out_specs, check_vma=False
    )
```

```python
import functools

import jax
import jax.numpy as jnp
from jax import lax
from jax.experimental import pallas as pl
from jax.experimental.pallas import tpu as pltpu
from jax.sharding import PartitionSpec as P

BF, F32 = jnp.bfloat16, jnp.float32
EARLIER = 6
RIM = 2


def call(body, outs, args, scratch=(), flops=0, name=None):
    spec = pl.BlockSpec(memory_space=pltpu.VMEM)
    outs = [jax.ShapeDtypeStruct(shape, kind) for shape, kind in outs]
    size = sum(a.size * a.dtype.itemsize for a in [*args, *outs])
    return pl.pallas_call(
        body, out_shape=outs, in_specs=[spec] * len(args), out_specs=[spec] * len(outs),
        scratch_shapes=[pltpu.VMEM(*s) for s in scratch], name=name,
        cost_estimate=pl.CostEstimate(flops=flops, bytes_accessed=size, transcendentals=0),
        compiler_params=pltpu.CompilerParams(vmem_limit_bytes=32 << 20),
    )(*args)


LANES = 128
SLACK = 8


def put(ref, rows, value, add=False):
    for k in range(ref.shape[0]):
        block = value[:, k * LANES : (k + 1) * LANES]
        ref[k, rows, :] = ref[k, rows, :] + block if add else block


def take(ref, rows, blocks=None):
    blocks = range(ref.shape[0]) if blocks is None else blocks
    return jnp.concatenate([ref[k, rows, :] for k in blocks], 1)


def blocked(rows, width):
    return (width // LANES, rows, LANES)


def swaps(size):
    assert size % 2 == 0
    rounds = [[(i, i + 1) for i in range(0, size, 2)]]
    if size > 2:
        rounds.append([(i, (i + 1) % size) for i in range(1, size, 2)])
    return [pairs + [(j, i) for i, j in pairs] for pairs in rounds]


def exchange(sends, axis):
    return [lax.ppermute(s, axis, pairs) for s, pairs in zip(sends, swaps(lax.axis_size(axis)))]


def arrived(axis, got):
    place, size = lax.axis_index(axis), lax.axis_size(axis)
    even = place % 2 == 0
    if len(got) == 1:
        before = after = got[0]
    else:
        before, after = jnp.where(even, got[1], got[0]), jnp.where(even, got[0], got[1])
    zero = jnp.zeros_like(before)
    return jnp.where(place > 0, before, zero), jnp.where(place < size - 1, after, zero)


def join_frames(*refs, pieces, rounds):
    own, got = refs[0], refs[1 : 1 + len(pieces)]
    field, sends = refs[1 + len(pieces)], refs[2 + len(pieces) :]
    place, at = lax.axis_index("section"), 0
    for (take, by), ref in zip(pieces, got):
        field[at : at + take] = jnp.where(place >= by, ref[...], jnp.zeros_like(ref))
        at += take
    field[at:] = own[...]
    even = lax.axis_index("row") % 2 == 0
    last = field.shape[1] - RIM
    for k in range(rounds):
        start = jnp.where(even, 0, last) if k else jnp.where(even, last, 0)
        sends[k][...] = field[:, pl.ds(start, RIM)]


def strips(*refs, rows):
    field, got = refs[0], refs[1 : 1 + rows]
    sends, wide = refs[1 + rows : -1], refs[-1]
    frames, height, breadth, width = field.shape
    before, after = arrived("row", [g[...].astype(F32) for g in got])
    tall = height + 2 * RIM
    for t in range(frames):
        whole = jnp.concatenate([before[t], field[t].astype(F32), after[t]], 0)
        size = tall * breadth
        put(wide, slice(t * size, (t + 1) * size), whole.reshape(size, width))
    first, last = (
        [take(wide, pl.ds(c, frames * tall, stride=breadth)).astype(BF) for c in cols]
        for cols in ([0, 1], [breadth - 2, breadth - 1])
    )
    even = lax.axis_index("col") % 2 == 0
    for k, send in enumerate(sends):
        for i in range(RIM):
            send[i] = jnp.where(even, first[i], last[i]) if k else jnp.where(even, last[i], first[i])


def first_inner(*refs, rows):
    field, got, kernel, out, wide = refs[0], refs[1 : 1 + rows], refs[1 + rows], refs[-2], refs[-1]
    frames, height, breadth, width = field.shape
    before, after = arrived("row", [g[...] for g in got])
    tall = height + 2 * RIM
    size = tall * breadth
    col = lax.broadcasted_iota(jnp.int32, (size, width), 0) % breadth
    for t in range(frames):
        whole = jnp.concatenate([before[t], field[t], after[t]], 0)
        wide[1, t] = whole
        flat = whole.reshape(size, width).astype(F32)
        lower = jnp.where(col == 0, 0.0, pltpu.roll(flat, 1, 0))
        upper = jnp.where(col == breadth - 1, 0.0, pltpu.roll(flat, size - 1, 0))
        wide[0, t] = lower.astype(BF).reshape(whole.shape)
        wide[2, t] = upper.astype(BF).reshape(whole.shape)
    taps = [
        wide[e, a : a + frames - 2, b : b + tall - 2].reshape(-1, width)
        for a in range(3) for b in range(3) for e in range(3)
    ]
    found = jnp.dot(
        jnp.concatenate(taps, 1), kernel[...].reshape(-1, kernel.shape[-1]), preferred_element_type=F32
    )
    out[...] = found.reshape(out.shape)


def kernels(second, third, summed, paired):
    fine = second.shape[-1]
    reads = [[(0, 1), (2,)], [(0,), (1, 2)]]
    for a in range(3):
        tap = [[second[a, b, e].astype(F32) for e in range(3)] for b in range(3)]
        for di in range(2):
            for dj in range(2):
                for py in range(2):
                    for px in range(2):
                        parts = [tap[b][e] for b in reads[py][di] for e in reads[px][dj]]
                        at = (2 * py + px) * fine
                        summed[a, di, dj, :, at : at + fine] = sum(parts[1:], parts[0]).astype(BF)
    width, out = third.shape[-2:]
    for a in range(3):
        for b in range(3):
            for dj in range(2):
                for px in range(2):
                    for q in range(2):
                        e = 2 * dj + px - q
                        block = third[a, b, e] if 0 <= e < 3 else jnp.zeros((width, out), BF)
                        paired[a, b, dj, px * width : (px + 1) * width, q * out : (q + 1) * out] = block


def rest(*refs, cols):
    inner, sent, got = refs[0], refs[1 : 1 + cols], refs[1 + cols : 1 + 2 * cols]
    kernel, summed, paired, out = refs[1 + 2 * cols : 5 + 2 * cols]
    edge, coarse, near, far, grown, fine, spread = refs[5 + 2 * cols :]
    frames, rows, breadth, width = inner.shape
    tall = rows + 2
    top, bottom = lax.axis_index("row") == 0, lax.axis_index("row") == lax.axis_size("row") - 1
    leftmost, rightmost = lax.axis_index("col") == 0, lax.axis_index("col") == lax.axis_size("col") - 1

    even = lax.axis_index("col") % 2 == 0
    before, after = arrived("col", [g[...] for g in got])
    if cols == 1:
        own = [sent[0][0], sent[0][1]]
    else:
        own = [jnp.where(even, sent[1][0], sent[0][0]), jnp.where(even, sent[0][1], sent[1][1])]
    size, count = frames * tall, before.shape[1]
    for i, strip in enumerate([before[0], before[1], own[0], own[1], after[0], after[1]]):
        edge[i, :count] = strip.astype(F32)

    def part(e, places):
        lhs = jnp.concatenate([
            jnp.concatenate(
                [edge[i, a * tall + b : a * tall + b + size].astype(BF) for i in places], 0
            )
            for a in range(3) for b in range(3)
        ], 1)
        rhs = jnp.concatenate([kernel[a, b, e] for a in range(3) for b in range(3)], 0)
        found = jnp.dot(lhs, rhs, preferred_element_type=F32)
        return [found[i * size : (i + 1) * size] for i in range(len(places))]

    left0, fix0, right0 = part(0, [0, 1, 3])
    left1, right1 = part(1, [1, 4])
    left2, fix1, right2 = part(2, [2, 4, 5])
    left, right = left0 + left1 + left2, right0 + right1 + right2

    pitch = breadth + SLACK
    for t in range(frames):
        for r in range(rows):
            at = (t * tall + r) * pitch
            put(coarse, slice(at, at + breadth), inner[t, r])
    put(coarse, pl.ds(0, size, stride=pitch), fix0, add=True)
    put(coarse, pl.ds(breadth - 1, size, stride=pitch), fix1, add=True)
    put(coarse, pl.ds(breadth, size, stride=pitch), right)
    begin = take(coarse, pl.ds(0, size, stride=pitch))

    def outside(row):
        return (top & (row == 0)) | (bottom & (row == rows - 1))

    slot = lax.broadcasted_iota(jnp.int32, (breadth, width), 0)
    ends = rightmost & (slot == breadth - 1)
    for t in range(frames):
        for r in range(rows):
            at = (t * tall + r) * pitch
            lost = top if r == 0 else bottom if r == rows - 1 else None
            for dj in range(2):
                value = jnp.maximum(take(coarse, slice(at + dj, at + dj + breadth)), 0.0)
                gone = [g for g in (lost, ends if dj else None) if g is not None]
                if gone:
                    value = jnp.where(functools.reduce(jnp.logical_or, gone), 0.0, value)
                near[dj, t, r] = value.astype(BF)
    row = lax.broadcasted_iota(jnp.int32, (size, width), 0) % tall
    far[0, :size] = jnp.where(outside(row) | leftmost, 0.0, jnp.maximum(left, 0.0))
    far[1, :size] = jnp.where(outside(row), 0.0, jnp.maximum(begin, 0.0))

    corners, later = rows - 1, frames - 2
    short = later * tall
    taps = [
        jnp.concatenate([
            near[dj, a : a + later, di : di + corners].reshape(-1, width),
            far[dj, a * tall + di : a * tall + di + short].astype(BF),
        ], 0)
        for a in range(3) for di in range(2) for dj in range(2)
    ]
    found = jnp.dot(
        jnp.concatenate(taps, 1), summed[...].reshape(-1, summed.shape[-1]), preferred_element_type=F32
    )
    found = jnp.maximum(found, 0.0)
    full = later * corners * breadth
    half = found.shape[1] // 2
    for t in range(later):
        for i in range(corners):
            at, to = (t * corners + i) * breadth, (t * tall + i) * pitch + SLACK
            put(grown, slice(to, to + breadth), found[at : at + breadth])
    put(grown, pl.ds(SLACK - 1, short, stride=pitch), found[full:])
    slot = lax.broadcasted_iota(jnp.int32, (breadth, half), 0)
    side = lax.broadcasted_iota(jnp.int32, (breadth, half), 1) < half // 2
    begins = leftmost & (slot == 0) & side
    ends = rightmost & (slot == breadth - 1) & ~side
    for t in range(later):
        for i in range(corners):
            for py in range(2):
                blocks = range(py * half // LANES, (py + 1) * half // LANES)
                lost = (top if py == 0 and i == 0 else bottom if py == 1 and i == corners - 1 else None)
                for dj, gone in enumerate((begins, ends)):
                    gone = gone if lost is None else gone | lost
                    at = (t * tall + i) * pitch + SLACK - 1 + dj
                    value = take(grown, slice(at, at + breadth), blocks)
                    fine[dj, 2 * i + py, t] = jnp.where(gone, 0.0, value).astype(BF)

    high, kept, wide = 2 * corners - 2, later - 2, out.shape[-1]
    taps = [
        fine[dj, b : b + high, a : a + kept].reshape(-1, half)
        for a in range(3) for b in range(3) for dj in range(2)
    ]
    found = jnp.dot(
        jnp.concatenate(taps, 1), paired[...].reshape(-1, paired.shape[-1]), preferred_element_type=F32
    )
    for y in range(high):
        for t in range(kept):
            at = (y * kept + t) * breadth
            for q in range(2):
                spread[t, y, pl.ds(q, breadth, stride=2), :] = found[
                    at : at + breadth, q * wide : (q + 1) * wide
                ]
    out[...] = spread[...].astype(BF)


def per_device(latent, w_first, w_second, w_third):
    frames, height, breadth, width = latent.shape
    mid, fine = w_first.shape[-1], w_second.shape[-1]
    last = w_third.shape[-1]
    sections = lax.axis_size("section")
    pieces, got, left, by = [], [], EARLIER, 1
    while left > 0:
        take = min(left, frames)
        ring = [(i, (i + by) % sections) for i in range(sections)]
        got.insert(0, lax.ppermute(latent[frames - take :], "section", ring))
        pieces.insert(0, (take, by))
        left, by = left - take, by + 1
    summed, paired = call(
        kernels, [((3, 2, 2, mid, 4 * fine), BF), ((3, 3, 2, 2 * fine, 2 * last), BF)],
        [w_second, w_third], name="kernels",
    )
    total = frames + EARLIER
    rounds = len(swaps(lax.axis_size("row")))
    field, *sends = call(
        functools.partial(join_frames, pieces=pieces, rounds=rounds),
        [((total, height, breadth, width), BF)] + [((total, RIM, breadth, width), BF)] * rounds,
        [latent, *got], name="join_frames",
    )
    rows_got = exchange(sends, "row")
    tall = height + 2 * RIM
    cols = len(swaps(lax.axis_size("col")))
    sends = call(
        functools.partial(strips, rows=rounds), [((RIM, total * tall, width), BF)] * cols,
        [field, *rows_got], [(blocked(total * tall * breadth, width), F32)], name="strips",
    )
    cols_got = exchange(sends, "col")
    early = total - 2
    (inner,) = call(
        functools.partial(first_inner, rows=rounds), [((early, tall - 2, breadth, mid), F32)],
        [field, *rows_got, w_first], [((3, total, tall, breadth, width), BF)],
        flops=2 * 27 * early * (tall - 2) * breadth * width * mid, name="first_inner",
    )
    later, corners = early - 2, tall - 3
    size = early * tall
    (out,) = call(
        functools.partial(rest, cols=cols), [((frames, 2 * height, 2 * breadth, last), BF)],
        [inner, *sends, *cols_got, w_first, summed, paired],
        [
            ((6, total * tall + 8, width), F32),
            (blocked(size * (breadth + SLACK), mid), F32),
            ((2, early, tall - 2, breadth, mid), BF),
            ((2, size + 8, mid), F32),
            (blocked(later * tall * (breadth + SLACK), 4 * fine), F32),
            ((2, 2 * corners, later, breadth, 2 * fine), BF),
            ((frames, 2 * height, 2 * breadth, last), F32),
        ],
        flops=4 * 10**9, name="rest",
    )
    return out


def solution(mesh):
    in_specs = (P("section", "row", "col", None), P(), P(), P())
    out_specs = P("section", "row", "col", None)
    return jax.shard_map(
        per_device, mesh=mesh, in_specs=in_specs, out_specs=out_specs, check_vma=False
    )
```

```python
import functools

import jax
import jax.numpy as jnp
from jax import lax
from jax.experimental import pallas as pl
from jax.experimental.pallas import tpu as pltpu
from jax.sharding import PartitionSpec as P

BF, F32 = jnp.bfloat16, jnp.float32
EARLIER = 6
RIM = 2


def call(body, outs, args, scratch=(), flops=0, name=None, space=pltpu.VMEM):
    spec = pl.BlockSpec(memory_space=pltpu.VMEM)
    outs = [jax.ShapeDtypeStruct(shape, kind) for shape, kind in outs]
    size = sum(a.size * a.dtype.itemsize for a in [*args, *outs])
    return pl.pallas_call(
        body, out_shape=outs, in_specs=[pl.BlockSpec(memory_space=space)] * len(args), out_specs=[spec] * len(outs),
        scratch_shapes=[pltpu.VMEM(*s) if isinstance(s, tuple) else s for s in scratch], name=name,
        cost_estimate=pl.CostEstimate(flops=flops, bytes_accessed=size, transcendentals=0),
        compiler_params=pltpu.CompilerParams(vmem_limit_bytes=32 << 20),
    )(*args)


LANES = 128
SLACK = 8


def put(ref, rows, value, add=False):
    for k in range(ref.shape[0]):
        block = value[:, k * LANES : (k + 1) * LANES]
        ref[k, rows, :] = ref[k, rows, :] + block if add else block


def take(ref, rows, blocks=None):
    blocks = range(ref.shape[0]) if blocks is None else blocks
    return jnp.concatenate([ref[k, rows, :] for k in blocks], 1)


def blocked(rows, width):
    return (width // LANES, rows, LANES)


def swaps(size):
    assert size % 2 == 0
    rounds = [[(i, i + 1) for i in range(0, size, 2)]]
    if size > 2:
        rounds.append([(i, (i + 1) % size) for i in range(1, size, 2)])
    return [pairs + [(j, i) for i, j in pairs] for pairs in rounds]


def exchange(sends, axis):
    return [lax.ppermute(s, axis, pairs) for s, pairs in zip(sends, swaps(lax.axis_size(axis)))]


def arrived(axis, got):
    place, size = lax.axis_index(axis), lax.axis_size(axis)
    even = place % 2 == 0
    if len(got) == 1:
        before = after = got[0]
    else:
        before, after = jnp.where(even, got[1], got[0]), jnp.where(even, got[0], got[1])
    zero = jnp.zeros_like(before)
    return jnp.where(place > 0, before, zero), jnp.where(place < size - 1, after, zero)


def join_frames(*refs, pieces, rounds):
    own, got = refs[0], refs[1 : 1 + len(pieces)]
    field, sends = refs[1 + len(pieces)], refs[2 + len(pieces) :]
    place, at = lax.axis_index("section"), 0
    for (take, by), ref in zip(pieces, got):
        field[at : at + take] = jnp.where(place >= by, ref[...], jnp.zeros_like(ref))
        at += take
    field[at:] = own[...]
    even = lax.axis_index("row") % 2 == 0
    last = field.shape[1] - RIM
    for k in range(rounds):
        start = jnp.where(even, 0, last) if k else jnp.where(even, last, 0)
        sends[k][...] = field[:, pl.ds(start, RIM)]


def strips(*refs, rows):
    field, got = refs[0], refs[1 : 1 + rows]
    sends, wide = refs[1 + rows : -1], refs[-1]
    frames, height, breadth, width = field.shape
    before, after = arrived("row", [g[...].astype(F32) for g in got])
    tall = height + 2 * RIM
    for t in range(frames):
        whole = jnp.concatenate([before[t], field[t].astype(F32), after[t]], 0)
        size = tall * breadth
        put(wide, slice(t * size, (t + 1) * size), whole.reshape(size, width))
    first, last = (
        [take(wide, pl.ds(c, frames * tall, stride=breadth)).astype(BF) for c in cols]
        for cols in ([0, 1], [breadth - 2, breadth - 1])
    )
    even = lax.axis_index("col") % 2 == 0
    for k, send in enumerate(sends):
        for i in range(RIM):
            send[i] = jnp.where(even, first[i], last[i]) if k else jnp.where(even, last[i], first[i])


def first_inner(*refs, rows):
    field, got, kernel, out, wide = refs[0], refs[1 : 1 + rows], refs[1 + rows], refs[-2], refs[-1]
    frames, height, breadth, width = field.shape
    before, after = arrived("row", [g[...] for g in got])
    tall = height + 2 * RIM
    size = tall * breadth
    col = lax.broadcasted_iota(jnp.int32, (size, width), 0) % breadth
    for t in range(frames):
        whole = jnp.concatenate([before[t], field[t], after[t]], 0)
        wide[1, t] = whole
        flat = whole.reshape(size, width).astype(F32)
        lower = jnp.where(col == 0, 0.0, pltpu.roll(flat, 1, 0))
        upper = jnp.where(col == breadth - 1, 0.0, pltpu.roll(flat, size - 1, 0))
        wide[0, t] = lower.astype(BF).reshape(whole.shape)
        wide[2, t] = upper.astype(BF).reshape(whole.shape)
    taps = [
        wide[e, a : a + frames - 2, b : b + tall - 2].reshape(-1, width)
        for a in range(3) for b in range(3) for e in range(3)
    ]
    found = jnp.dot(
        jnp.concatenate(taps, 1), kernel[...].reshape(-1, kernel.shape[-1]), preferred_element_type=F32
    )
    out[...] = found.reshape(out.shape)


def load(latent, first_from, second_from, third_from, own, first, summed, paired, second, third, sems):
    pairs = [(second_from.at[a], second.at[a]) for a in range(3)]
    pairs += [(third_from, third), (latent, own), (first_from, first)]
    copies = [pltpu.make_async_copy(*pair, sems.at[k]) for k, pair in enumerate(pairs)]
    for copy in copies:
        copy.start()
    fine = second.shape[-1]
    reads = [[(0, 1), (2,)], [(0,), (1, 2)]]
    for a in range(3):
        copies[a].wait()
        tap = [[second[a, b, e].astype(F32) for e in range(3)] for b in range(3)]
        for di in range(2):
            for dj in range(2):
                for py in range(2):
                    for px in range(2):
                        parts = [tap[b][e] for b in reads[py][di] for e in reads[px][dj]]
                        at = (2 * py + px) * fine
                        summed[a, di, dj, :, at : at + fine] = sum(parts[1:], parts[0]).astype(BF)
    width, out = third.shape[-2:]
    copies[3].wait()
    for a in range(3):
        for b in range(3):
            for dj in range(2):
                for px in range(2):
                    for q in range(2):
                        e = 2 * dj + px - q
                        block = third[a, b, e] if 0 <= e < 3 else jnp.zeros((width, out), BF)
                        paired[a, b, dj, px * width : (px + 1) * width, q * out : (q + 1) * out] = block
    copies[4].wait()
    copies[5].wait()


def rest(*refs, cols):
    inner, sent, got = refs[0], refs[1 : 1 + cols], refs[1 + cols : 1 + 2 * cols]
    kernel, summed, paired, out = refs[1 + 2 * cols : 5 + 2 * cols]
    edge, coarse, near, far, grown, fine, spread = refs[5 + 2 * cols :]
    frames, rows, breadth, width = inner.shape
    tall = rows + 2
    top, bottom = lax.axis_index("row") == 0, lax.axis_index("row") == lax.axis_size("row") - 1
    leftmost, rightmost = lax.axis_index("col") == 0, lax.axis_index("col") == lax.axis_size("col") - 1

    even = lax.axis_index("col") % 2 == 0
    before, after = arrived("col", [g[...] for g in got])
    if cols == 1:
        own = [sent[0][0], sent[0][1]]
    else:
        own = [jnp.where(even, sent[1][0], sent[0][0]), jnp.where(even, sent[0][1], sent[1][1])]
    size, count = frames * tall, before.shape[1]
    for i, strip in enumerate([before[0], before[1], own[0], own[1], after[0], after[1]]):
        edge[i, :count] = strip.astype(F32)

    def part(e, places):
        lhs = jnp.concatenate([
            jnp.concatenate(
                [edge[i, a * tall + b : a * tall + b + size].astype(BF) for i in places], 0
            )
            for a in range(3) for b in range(3)
        ], 1)
        rhs = jnp.concatenate([kernel[a, b, e] for a in range(3) for b in range(3)], 0)
        found = jnp.dot(lhs, rhs, preferred_element_type=F32)
        return [found[i * size : (i + 1) * size] for i in range(len(places))]

    left0, fix0, right0 = part(0, [0, 1, 3])
    left1, right1 = part(1, [1, 4])
    left2, fix1, right2 = part(2, [2, 4, 5])
    left, right = left0 + left1 + left2, right0 + right1 + right2

    pitch = breadth + SLACK
    for t in range(frames):
        for r in range(rows):
            at = (t * tall + r) * pitch
            put(coarse, slice(at, at + breadth), inner[t, r])
    put(coarse, pl.ds(0, size, stride=pitch), fix0, add=True)
    put(coarse, pl.ds(breadth - 1, size, stride=pitch), fix1, add=True)
    put(coarse, pl.ds(breadth, size, stride=pitch), right)
    begin = take(coarse, pl.ds(0, size, stride=pitch))

    def outside(row):
        return (top & (row == 0)) | (bottom & (row == rows - 1))

    slot = lax.broadcasted_iota(jnp.int32, (breadth, width), 0)
    ends = rightmost & (slot == breadth - 1)
    for t in range(frames):
        for r in range(rows):
            at = (t * tall + r) * pitch
            lost = top if r == 0 else bottom if r == rows - 1 else None
            for dj in range(2):
                value = jnp.maximum(take(coarse, slice(at + dj, at + dj + breadth)), 0.0)
                gone = [g for g in (lost, ends if dj else None) if g is not None]
                if gone:
                    value = jnp.where(functools.reduce(jnp.logical_or, gone), 0.0, value)
                near[dj, t, r] = value.astype(BF)
    row = lax.broadcasted_iota(jnp.int32, (size, width), 0) % tall
    far[0, :size] = jnp.where(outside(row) | leftmost, 0.0, jnp.maximum(left, 0.0))
    far[1, :size] = jnp.where(outside(row), 0.0, jnp.maximum(begin, 0.0))

    corners, later = rows - 1, frames - 2
    short = later * tall
    taps = [
        jnp.concatenate([
            near[dj, a : a + later, di : di + corners].reshape(-1, width),
            far[dj, a * tall + di : a * tall + di + short].astype(BF),
        ], 0)
        for a in range(3) for di in range(2) for dj in range(2)
    ]
    found = jnp.dot(
        jnp.concatenate(taps, 1), summed[...].reshape(-1, summed.shape[-1]), preferred_element_type=F32
    )
    found = jnp.maximum(found, 0.0)
    full = later * corners * breadth
    half = found.shape[1] // 2
    for t in range(later):
        for i in range(corners):
            at, to = (t * corners + i) * breadth, (t * tall + i) * pitch + SLACK
            put(grown, slice(to, to + breadth), found[at : at + breadth])
    put(grown, pl.ds(SLACK - 1, short, stride=pitch), found[full:])
    slot = lax.broadcasted_iota(jnp.int32, (breadth, half), 0)
    side = lax.broadcasted_iota(jnp.int32, (breadth, half), 1) < half // 2
    begins = leftmost & (slot == 0) & side
    ends = rightmost & (slot == breadth - 1) & ~side
    for t in range(later):
        for i in range(corners):
            for py in range(2):
                blocks = range(py * half // LANES, (py + 1) * half // LANES)
                lost = (top if py == 0 and i == 0 else bottom if py == 1 and i == corners - 1 else None)
                for dj, gone in enumerate((begins, ends)):
                    gone = gone if lost is None else gone | lost
                    at = (t * tall + i) * pitch + SLACK - 1 + dj
                    value = take(grown, slice(at, at + breadth), blocks)
                    fine[dj, 2 * i + py, t] = jnp.where(gone, 0.0, value).astype(BF)

    high, kept, wide = 2 * corners - 2, later - 2, out.shape[-1]
    taps = [
        fine[dj, b : b + high, a : a + kept].reshape(-1, half)
        for a in range(3) for b in range(3) for dj in range(2)
    ]
    found = jnp.dot(
        jnp.concatenate(taps, 1), paired[...].reshape(-1, paired.shape[-1]), preferred_element_type=F32
    )
    for y in range(high):
        for t in range(kept):
            at = (y * kept + t) * breadth
            for q in range(2):
                spread[t, y, pl.ds(q, breadth, stride=2), :] = found[
                    at : at + breadth, q * wide : (q + 1) * wide
                ]
    out[...] = spread[...].astype(BF)


def per_device(latent, w_first, w_second, w_third):
    frames, height, breadth, width = latent.shape
    mid, fine = w_first.shape[-1], w_second.shape[-1]
    last = w_third.shape[-1]
    sections = lax.axis_size("section")
    pieces, got, left, by = [], [], EARLIER, 1
    while left > 0:
        take = min(left, frames)
        ring = [(i, (i + by) % sections) for i in range(sections)]
        got.insert(0, lax.ppermute(latent[frames - take :], "section", ring))
        pieces.insert(0, (take, by))
        left, by = left - take, by + 1
    latent, w_first, summed, paired = call(
        load,
        [
            (latent.shape, BF), (w_first.shape, BF),
            ((3, 2, 2, mid, 4 * fine), BF), ((3, 3, 2, 2 * fine, 2 * last), BF),
        ],
        [latent, w_first, w_second, w_third],
        [(w_second.shape, BF), (w_third.shape, BF), pltpu.SemaphoreType.DMA((6,))],
        name="load", space=pltpu.HBM,
    )
    total = frames + EARLIER
    rounds = len(swaps(lax.axis_size("row")))
    field, *sends = call(
        functools.partial(join_frames, pieces=pieces, rounds=rounds),
        [((total, height, breadth, width), BF)] + [((total, RIM, breadth, width), BF)] * rounds,
        [latent, *got], name="join_frames",
    )
    rows_got = exchange(sends, "row")
    tall = height + 2 * RIM
    cols = len(swaps(lax.axis_size("col")))
    sends = call(
        functools.partial(strips, rows=rounds), [((RIM, total * tall, width), BF)] * cols,
        [field, *rows_got], [(blocked(total * tall * breadth, width), F32)], name="strips",
    )
    cols_got = exchange(sends, "col")
    early = total - 2
    (inner,) = call(
        functools.partial(first_inner, rows=rounds), [((early, tall - 2, breadth, mid), F32)],
        [field, *rows_got, w_first], [((3, total, tall, breadth, width), BF)],
        flops=2 * 27 * early * (tall - 2) * breadth * width * mid, name="first_inner",
    )
    later, corners = early - 2, tall - 3
    size = early * tall
    (out,) = call(
        functools.partial(rest, cols=cols), [((frames, 2 * height, 2 * breadth, last), BF)],
        [inner, *sends, *cols_got, w_first, summed, paired],
        [
            ((6, total * tall + 8, width), F32),
            (blocked(size * (breadth + SLACK), mid), F32),
            ((2, early, tall - 2, breadth, mid), BF),
            ((2, size + 8, mid), F32),
            (blocked(later * tall * (breadth + SLACK), 4 * fine), F32),
            ((2, 2 * corners, later, breadth, 2 * fine), BF),
            ((frames, 2 * height, 2 * breadth, last), F32),
        ],
        flops=4 * 10**9, name="rest",
    )
    return out


def solution(mesh):
    in_specs = (P("section", "row", "col", None), P(), P(), P())
    out_specs = P("section", "row", "col", None)
    return jax.shard_map(
        per_device, mesh=mesh, in_specs=in_specs, out_specs=out_specs, check_vma=False
    )
```

```python
import functools

import jax
import jax.numpy as jnp
from jax import lax
from jax.experimental import pallas as pl
from jax.experimental.pallas import tpu as pltpu
from jax.sharding import PartitionSpec as P

BF, F32 = jnp.bfloat16, jnp.float32
EARLIER = 6
RIM = 2


def call(body, outs, args, scratch=(), flops=0, name=None):
    spec = pl.BlockSpec(memory_space=pltpu.VMEM)
    outs = [jax.ShapeDtypeStruct(shape, kind) for shape, kind in outs]
    size = sum(a.size * a.dtype.itemsize for a in [*args, *outs])
    return pl.pallas_call(
        body, out_shape=outs, in_specs=[spec] * len(args), out_specs=[spec] * len(outs),
        scratch_shapes=[pltpu.VMEM(*s) for s in scratch], name=name,
        cost_estimate=pl.CostEstimate(flops=flops, bytes_accessed=size, transcendentals=0),
        compiler_params=pltpu.CompilerParams(vmem_limit_bytes=32 << 20),
    )(*args)


LANES = 128
COVER = 4 * 10**9
SLACK = 8


def put(ref, rows, value, add=False):
    for k in range(ref.shape[0]):
        block = value[:, k * LANES : (k + 1) * LANES]
        ref[k, rows, :] = ref[k, rows, :] + block if add else block


def take(ref, rows, blocks=None):
    blocks = range(ref.shape[0]) if blocks is None else blocks
    return jnp.concatenate([ref[k, rows, :] for k in blocks], 1)


def blocked(rows, width):
    return (width // LANES, rows, LANES)


def swaps(size):
    assert size % 2 == 0
    rounds = [[(i, i + 1) for i in range(0, size, 2)]]
    if size > 2:
        rounds.append([(i, (i + 1) % size) for i in range(1, size, 2)])
    return [pairs + [(j, i) for i, j in pairs] for pairs in rounds]


def exchange(sends, axis):
    return [lax.ppermute(s, axis, pairs) for s, pairs in zip(sends, swaps(lax.axis_size(axis)))]


def arrived(axis, got):
    place, size = lax.axis_index(axis), lax.axis_size(axis)
    even = place % 2 == 0
    if len(got) == 1:
        before = after = got[0]
    else:
        before, after = jnp.where(even, got[1], got[0]), jnp.where(even, got[0], got[1])
    zero = jnp.zeros_like(before)
    return jnp.where(place > 0, before, zero), jnp.where(place < size - 1, after, zero)


def join_frames(*refs, pieces, rounds):
    own, got = refs[0], refs[2 : 2 + len(pieces)]
    field, sends = refs[2 + len(pieces)], refs[3 + len(pieces) :]
    place, at = lax.axis_index("section"), 0
    for (take, by), ref in zip(pieces, got):
        field[at : at + take] = jnp.where(place >= by, ref[...], jnp.zeros_like(ref))
        at += take
    field[at:] = own[...]
    even = lax.axis_index("row") % 2 == 0
    last = field.shape[1] - RIM
    for k in range(rounds):
        start = jnp.where(even, 0, last) if k else jnp.where(even, last, 0)
        sends[k][...] = field[:, pl.ds(start, RIM)]


def strips(*refs, rows):
    field, got = refs[0], refs[1 : 1 + rows]
    sends, wide = refs[1 + rows : -1], refs[-1]
    frames, height, breadth, width = field.shape
    before, after = arrived("row", [g[...].astype(F32) for g in got])
    tall = height + 2 * RIM
    for t in range(frames):
        whole = jnp.concatenate([before[t], field[t].astype(F32), after[t]], 0)
        size = tall * breadth
        put(wide, slice(t * size, (t + 1) * size), whole.reshape(size, width))
    first, last = (
        [take(wide, pl.ds(c, frames * tall, stride=breadth)).astype(BF) for c in cols]
        for cols in ([0, 1], [breadth - 2, breadth - 1])
    )
    even = lax.axis_index("col") % 2 == 0
    for k, send in enumerate(sends):
        for i in range(RIM):
            send[i] = jnp.where(even, first[i], last[i]) if k else jnp.where(even, last[i], first[i])


def first_inner(*refs, rows):
    field, got, kernel, out, wide = refs[0], refs[1 : 1 + rows], refs[1 + rows], refs[-2], refs[-1]
    frames, height, breadth, width = field.shape
    before, after = arrived("row", [g[...] for g in got])
    tall = height + 2 * RIM
    size = tall * breadth
    col = lax.broadcasted_iota(jnp.int32, (size, width), 0) % breadth
    for t in range(frames):
        whole = jnp.concatenate([before[t], field[t], after[t]], 0)
        wide[1, t] = whole
        flat = whole.reshape(size, width).astype(F32)
        lower = jnp.where(col == 0, 0.0, pltpu.roll(flat, 1, 0))
        upper = jnp.where(col == breadth - 1, 0.0, pltpu.roll(flat, size - 1, 0))
        wide[0, t] = lower.astype(BF).reshape(whole.shape)
        wide[2, t] = upper.astype(BF).reshape(whole.shape)
    taps = [
        wide[e, a : a + frames - 2, b : b + tall - 2].reshape(-1, width)
        for a in range(3) for b in range(3) for e in range(3)
    ]
    found = jnp.dot(
        jnp.concatenate(taps, 1), kernel[...].reshape(-1, kernel.shape[-1]), preferred_element_type=F32
    )
    out[...] = found.reshape(out.shape)


def kernels(second, third, summed, paired, ready):
    ready[...] = jnp.zeros_like(ready)
    fine = second.shape[-1]
    reads = [[(0, 1), (2,)], [(0,), (1, 2)]]
    for a in range(3):
        tap = [[second[a, b, e].astype(F32) for e in range(3)] for b in range(3)]
        for di in range(2):
            for dj in range(2):
                for py in range(2):
                    for px in range(2):
                        parts = [tap[b][e] for b in reads[py][di] for e in reads[px][dj]]
                        at = (2 * py + px) * fine
                        summed[a, di, dj, :, at : at + fine] = sum(parts[1:], parts[0]).astype(BF)
    width, out = third.shape[-2:]
    for a in range(3):
        for b in range(3):
            for dj in range(2):
                for px in range(2):
                    for q in range(2):
                        e = 2 * dj + px - q
                        block = third[a, b, e] if 0 <= e < 3 else jnp.zeros((width, out), BF)
                        paired[a, b, dj, px * width : (px + 1) * width, q * out : (q + 1) * out] = block


def rest(*refs, cols):
    inner, sent, got = refs[0], refs[1 : 1 + cols], refs[1 + cols : 1 + 2 * cols]
    kernel, summed, paired, out = refs[1 + 2 * cols : 5 + 2 * cols]
    edge, coarse, near, far, grown, fine, spread = refs[5 + 2 * cols :]
    frames, rows, breadth, width = inner.shape
    tall = rows + 2
    top, bottom = lax.axis_index("row") == 0, lax.axis_index("row") == lax.axis_size("row") - 1
    leftmost, rightmost = lax.axis_index("col") == 0, lax.axis_index("col") == lax.axis_size("col") - 1

    even = lax.axis_index("col") % 2 == 0
    before, after = arrived("col", [g[...] for g in got])
    if cols == 1:
        own = [sent[0][0], sent[0][1]]
    else:
        own = [jnp.where(even, sent[1][0], sent[0][0]), jnp.where(even, sent[0][1], sent[1][1])]
    size, count = frames * tall, before.shape[1]
    for i, strip in enumerate([before[0], before[1], own[0], own[1], after[0], after[1]]):
        edge[i, :count] = strip.astype(F32)

    def part(e, places):
        lhs = jnp.concatenate([
            jnp.concatenate(
                [edge[i, a * tall + b : a * tall + b + size].astype(BF) for i in places], 0
            )
            for a in range(3) for b in range(3)
        ], 1)
        rhs = jnp.concatenate([kernel[a, b, e] for a in range(3) for b in range(3)], 0)
        found = jnp.dot(lhs, rhs, preferred_element_type=F32)
        return [found[i * size : (i + 1) * size] for i in range(len(places))]

    left0, fix0, right0 = part(0, [0, 1, 3])
    left1, right1 = part(1, [1, 4])
    left2, fix1, right2 = part(2, [2, 4, 5])
    left, right = left0 + left1 + left2, right0 + right1 + right2

    pitch = breadth + SLACK
    for t in range(frames):
        for r in range(rows):
            at = (t * tall + r) * pitch
            put(coarse, slice(at, at + breadth), inner[t, r])
    put(coarse, pl.ds(0, size, stride=pitch), fix0, add=True)
    put(coarse, pl.ds(breadth - 1, size, stride=pitch), fix1, add=True)
    put(coarse, pl.ds(breadth, size, stride=pitch), right)
    begin = take(coarse, pl.ds(0, size, stride=pitch))

    def outside(row):
        return (top & (row == 0)) | (bottom & (row == rows - 1))

    slot = lax.broadcasted_iota(jnp.int32, (breadth, width), 0)
    ends = rightmost & (slot == breadth - 1)
    for t in range(frames):
        for r in range(rows):
            at = (t * tall + r) * pitch
            lost = top if r == 0 else bottom if r == rows - 1 else None
            for dj in range(2):
                value = jnp.maximum(take(coarse, slice(at + dj, at + dj + breadth)), 0.0)
                gone = [g for g in (lost, ends if dj else None) if g is not None]
                if gone:
                    value = jnp.where(functools.reduce(jnp.logical_or, gone), 0.0, value)
                near[dj, t, r] = value.astype(BF)
    row = lax.broadcasted_iota(jnp.int32, (size, width), 0) % tall
    far[0, :size] = jnp.where(outside(row) | leftmost, 0.0, jnp.maximum(left, 0.0))
    far[1, :size] = jnp.where(outside(row), 0.0, jnp.maximum(begin, 0.0))

    corners, later = rows - 1, frames - 2
    short = later * tall
    taps = [
        jnp.concatenate([
            near[dj, a : a + later, di : di + corners].reshape(-1, width),
            far[dj, a * tall + di : a * tall + di + short].astype(BF),
        ], 0)
        for a in range(3) for di in range(2) for dj in range(2)
    ]
    found = jnp.dot(
        jnp.concatenate(taps, 1), summed[...].reshape(-1, summed.shape[-1]), preferred_element_type=F32
    )
    found = jnp.maximum(found, 0.0)
    full = later * corners * breadth
    half = found.shape[1] // 2
    for t in range(later):
        for i in range(corners):
            at, to = (t * corners + i) * breadth, (t * tall + i) * pitch + SLACK
            put(grown, slice(to, to + breadth), found[at : at + breadth])
    put(grown, pl.ds(SLACK - 1, short, stride=pitch), found[full:])
    slot = lax.broadcasted_iota(jnp.int32, (breadth, half), 0)
    side = lax.broadcasted_iota(jnp.int32, (breadth, half), 1) < half // 2
    begins = leftmost & (slot == 0) & side
    ends = rightmost & (slot == breadth - 1) & ~side
    for t in range(later):
        for i in range(corners):
            for py in range(2):
                blocks = range(py * half // LANES, (py + 1) * half // LANES)
                lost = (top if py == 0 and i == 0 else bottom if py == 1 and i == corners - 1 else None)
                for dj, gone in enumerate((begins, ends)):
                    gone = gone if lost is None else gone | lost
                    at = (t * tall + i) * pitch + SLACK - 1 + dj
                    value = take(grown, slice(at, at + breadth), blocks)
                    fine[dj, 2 * i + py, t] = jnp.where(gone, 0.0, value).astype(BF)

    high, kept, wide = 2 * corners - 2, later - 2, out.shape[-1]
    taps = [
        fine[dj, b : b + high, a : a + kept].reshape(-1, half)
        for a in range(3) for b in range(3) for dj in range(2)
    ]
    found = jnp.dot(
        jnp.concatenate(taps, 1), paired[...].reshape(-1, paired.shape[-1]), preferred_element_type=F32
    )
    for y in range(high):
        for t in range(kept):
            at = (y * kept + t) * breadth
            for q in range(2):
                spread[t, y, pl.ds(q, breadth, stride=2), :] = found[
                    at : at + breadth, q * wide : (q + 1) * wide
                ]
    out[...] = spread[...].astype(BF)


def per_device(latent, w_first, w_second, w_third):
    frames, height, breadth, width = latent.shape
    mid, fine = w_first.shape[-1], w_second.shape[-1]
    last = w_third.shape[-1]
    sections = lax.axis_size("section")
    pieces, got, left, by = [], [], EARLIER, 1
    while left > 0:
        take = min(left, frames)
        ring = [(i, (i + by) % sections) for i in range(sections)]
        got.insert(0, lax.ppermute(latent[frames - take :], "section", ring))
        pieces.insert(0, (take, by))
        left, by = left - take, by + 1
    summed, paired, ready = call(
        kernels,
        [((3, 2, 2, mid, 4 * fine), BF), ((3, 3, 2, 2 * fine, 2 * last), BF), ((8, LANES), F32)],
        [w_second, w_third], flops=COVER, name="kernels",
    )
    total = frames + EARLIER
    rounds = len(swaps(lax.axis_size("row")))
    field, *sends = call(
        functools.partial(join_frames, pieces=pieces, rounds=rounds),
        [((total, height, breadth, width), BF)] + [((total, RIM, breadth, width), BF)] * rounds,
        [latent, ready, *got], flops=COVER, name="join_frames",
    )
    rows_got = exchange(sends, "row")
    tall = height + 2 * RIM
    cols = len(swaps(lax.axis_size("col")))
    sends = call(
        functools.partial(strips, rows=rounds), [((RIM, total * tall, width), BF)] * cols,
        [field, *rows_got], [(blocked(total * tall * breadth, width), F32)], name="strips",
    )
    cols_got = exchange(sends, "col")
    early = total - 2
    (inner,) = call(
        functools.partial(first_inner, rows=rounds), [((early, tall - 2, breadth, mid), F32)],
        [field, *rows_got, w_first], [((3, total, tall, breadth, width), BF)],
        flops=2 * 27 * early * (tall - 2) * breadth * width * mid, name="first_inner",
    )
    later, corners = early - 2, tall - 3
    size = early * tall
    (out,) = call(
        functools.partial(rest, cols=cols), [((frames, 2 * height, 2 * breadth, last), BF)],
        [inner, *sends, *cols_got, w_first, summed, paired],
        [
            ((6, total * tall + 8, width), F32),
            (blocked(size * (breadth + SLACK), mid), F32),
            ((2, early, tall - 2, breadth, mid), BF),
            ((2, size + 8, mid), F32),
            (blocked(later * tall * (breadth + SLACK), 4 * fine), F32),
            ((2, 2 * corners, later, breadth, 2 * fine), BF),
            ((frames, 2 * height, 2 * breadth, last), F32),
        ],
        flops=4 * 10**9, name="rest",
    )
    return out


def solution(mesh):
    in_specs = (P("section", "row", "col", None), P(), P(), P())
    out_specs = P("section", "row", "col", None)
    return jax.shard_map(
        per_device, mesh=mesh, in_specs=in_specs, out_specs=out_specs, check_vma=False
    )
```

```python
import functools

import jax
import jax.numpy as jnp
from jax import lax
from jax.experimental import pallas as pl
from jax.experimental.pallas import tpu as pltpu
from jax.sharding import PartitionSpec as P

BF, F32 = jnp.bfloat16, jnp.float32
EARLIER = 6
RIM = 2


def call(body, outs, args, scratch=(), flops=0, name=None):
    spec = pl.BlockSpec(memory_space=pltpu.VMEM)
    outs = [jax.ShapeDtypeStruct(shape, kind) for shape, kind in outs]
    size = sum(a.size * a.dtype.itemsize for a in [*args, *outs])
    return pl.pallas_call(
        body, out_shape=outs, in_specs=[spec] * len(args), out_specs=[spec] * len(outs),
        scratch_shapes=[pltpu.VMEM(*s) for s in scratch], name=name,
        cost_estimate=pl.CostEstimate(flops=flops, bytes_accessed=size, transcendentals=0),
        compiler_params=pltpu.CompilerParams(vmem_limit_bytes=32 << 20),
    )(*args)


LANES = 128
COVER = 4 * 10**9
SLACK = 8


def put(ref, rows, value):
    for k in range(ref.shape[0]):
        ref[k, rows, :] = value[:, k * LANES : (k + 1) * LANES]


def take(ref, rows, blocks=None):
    blocks = range(ref.shape[0]) if blocks is None else blocks
    return jnp.concatenate([ref[k, rows, :] for k in blocks], 1)


def blocked(rows, width):
    return (width // LANES, rows, LANES)


def swaps(size):
    assert size % 2 == 0
    rounds = [[(i, i + 1) for i in range(0, size, 2)]]
    if size > 2:
        rounds.append([(i, (i + 1) % size) for i in range(1, size, 2)])
    return [pairs + [(j, i) for i, j in pairs] for pairs in rounds]


def exchange(sends, axis):
    return [lax.ppermute(s, axis, pairs) for s, pairs in zip(sends, swaps(lax.axis_size(axis)))]


def arrived(axis, got):
    place, size = lax.axis_index(axis), lax.axis_size(axis)
    even = place % 2 == 0
    if len(got) == 1:
        before = after = got[0]
    else:
        before, after = jnp.where(even, got[1], got[0]), jnp.where(even, got[0], got[1])
    zero = jnp.zeros_like(before)
    return jnp.where(place > 0, before, zero), jnp.where(place < size - 1, after, zero)


def join_frames(*refs, pieces):
    own, got = refs[0], refs[2 : 2 + len(pieces)]
    field, sends = refs[2 + len(pieces)], refs[3 + len(pieces) :]
    place, at = lax.axis_index("section"), 0
    for (take, by), ref in zip(pieces, got):
        field[at : at + take] = jnp.where(place >= by, ref[...], jnp.zeros_like(ref))
        at += take
    field[at:] = own[...]
    even = lax.axis_index("row") % 2 == 0
    last = field.shape[1] - RIM
    for k in range(len(sends)):
        start = jnp.where(even, 0, last) if k else jnp.where(even, last, 0)
        sends[k][...] = field[:, pl.ds(start, RIM)]


def rims(field, got, whole):
    if whole:
        got = [jnp.where(lax.axis_index("row") == 0, got[0][:, :RIM], got[0][:, -RIM:])]
    else:
        got = [g[...] for g in got]
    return arrived("row", got)


def strips(*refs, rows, whole):
    field, got = refs[0], refs[1 : 1 + rows]
    sends, own, wide = refs[1 + rows : -2], refs[-2], refs[-1]
    frames, height, breadth, width = field.shape
    if whole:
        upper = lax.axis_index("row") == 0
    else:
        before, after = rims(field, got, whole)
    size = wide.shape[1] // frames
    tall = size // breadth
    for t in range(frames):
        if whole:
            a, b = field[t].astype(F32), got[0][t].astype(F32)
            rows_of = [jnp.where(upper, a, b), jnp.where(upper, b, a)]
        else:
            rows_of = [before[t].astype(F32), field[t].astype(F32), after[t].astype(F32)]
        put(wide, slice(t * size, (t + 1) * size), jnp.concatenate(rows_of, 0).reshape(size, width))
    for i, c in enumerate([0, 1, breadth - 2, breadth - 1]):
        own[i] = take(wide, pl.ds(c, frames * tall, stride=breadth)).astype(BF)
    right = lax.axis_index("col") % 2 == 0
    if whole:
        right = right == (lax.axis_index("row") == 0)
    for k, send in enumerate(sends):
        start = jnp.where(right, 0, RIM) if k else jnp.where(right, RIM, 0)
        send[...] = own[pl.ds(start, RIM)]


def first_inner(*refs, rows, whole, begin):
    field, got, kernel = refs[0], refs[1 : 1 + rows], refs[1 + rows]
    out, wide = refs[-2:]
    count = out.shape[0]
    _, height, breadth, width = field.shape
    before, after = rims(field, got, whole)
    tall = height + 2 * RIM
    size = tall * breadth
    col = lax.broadcasted_iota(jnp.int32, (size, width), 0) % breadth
    for t in range(count + 2):
        rows_of = jnp.concatenate([before[begin + t], field[begin + t], after[begin + t]], 0)
        wide[1, t] = rows_of
        flat = rows_of.reshape(size, width).astype(F32)
        lower = jnp.where(col == 0, 0.0, pltpu.roll(flat, 1, 0))
        upper = jnp.where(col == breadth - 1, 0.0, pltpu.roll(flat, size - 1, 0))
        wide[0, t] = lower.astype(BF).reshape(rows_of.shape)
        wide[2, t] = upper.astype(BF).reshape(rows_of.shape)
    taps = [
        wide[e, a : a + count, b : b + tall - 2].reshape(-1, width)
        for a in range(3) for b in range(3) for e in range(3)
    ]
    found = jnp.dot(
        jnp.concatenate(taps, 1), kernel[...].reshape(-1, kernel.shape[-1]), preferred_element_type=F32
    )
    out[...] = found.reshape(out.shape)


def kernels(second, third, summed, paired, ready):
    ready[...] = jnp.zeros_like(ready)
    fine = second.shape[-1]
    reads = [[(0, 1), (2,)], [(0,), (1, 2)]]
    for a in range(3):
        tap = [[second[a, b, e].astype(F32) for e in range(3)] for b in range(3)]
        for di in range(2):
            for dj in range(2):
                for py in range(2):
                    for px in range(2):
                        parts = [tap[b][e] for b in reads[py][di] for e in reads[px][dj]]
                        at = (2 * py + px) * fine
                        summed[a, di, dj, :, at : at + fine] = sum(parts[1:], parts[0]).astype(BF)
    width, out = third.shape[-2:]
    for a in range(3):
        for b in range(3):
            for dj in range(2):
                for px in range(2):
                    for q in range(2):
                        e = 2 * dj + px - q
                        block = third[a, b, e] if 0 <= e < 3 else jnp.zeros((width, out), BF)
                        paired[a, b, dj, px * width : (px + 1) * width, q * out : (q + 1) * out] = block


def rest(*refs, cols, parts, whole):
    inner, own, got = refs[:parts], refs[parts], refs[parts + 1 : parts + 1 + cols]
    kernel, summed, paired, out = refs[parts + 1 + cols : parts + 5 + cols]
    edge, coarse, near, far, grown, fine, spread = refs[parts + 5 + cols :]
    rows, breadth, width = inner[0].shape[1:]
    frames = sum(part.shape[0] for part in inner)
    tall = rows + 2
    top, bottom = lax.axis_index("row") == 0, lax.axis_index("row") == lax.axis_size("row") - 1
    leftmost, rightmost = lax.axis_index("col") == 0, lax.axis_index("col") == lax.axis_size("col") - 1

    got = [g[...] for g in got]
    if whole:
        got = [jnp.where(top, *got), jnp.where(top, *got[::-1])]
    before, after = arrived("col", got)
    size = frames * tall
    for i in range(RIM):
        edge[i], edge[RIM + i] = before[i], own[i]
        edge[2 * RIM + i], edge[3 * RIM + i] = own[RIM + i], after[i]
    lhs = jnp.concatenate([
        jnp.concatenate(
            [edge[i + e, a * tall : a * tall + size] for i in (0, 1, 4, 5)], 0
        )
        for a in range(3) for e in range(3)
    ], 1)
    rhs = jnp.concatenate([
        jnp.concatenate([kernel[a, b, e] for b in range(3)], 1) for a in range(3) for e in range(3)
    ], 0)
    found = jnp.dot(lhs, rhs, preferred_element_type=F32)
    row = lax.broadcasted_iota(jnp.int32, (size, width), 0) % tall

    def placed(i):
        total = 0.0
        for b in range(3):
            value = found[i * size : (i + 1) * size, b * width : (b + 1) * width]
            if whole:
                shift = jnp.where(top, -RIM, tall // 2 - RIM) + b
                value = pltpu.roll(value, jnp.where(shift > 0, size - shift, -shift), 0)
                value = jnp.where((row + shift >= 0) & (row + shift < tall), value, 0.0)
            elif b:
                value = pltpu.roll(value, size - b, 0)
            total = total + value
        return total

    left, begin, end, right = [placed(i) for i in range(4)]

    pitch = breadth + SLACK
    at = 0
    for part in inner:
        for t in range(part.shape[0]):
            for r in range(rows):
                put(coarse, slice(at + r * pitch, at + r * pitch + breadth), part[t, r])
            at += tall * pitch
    put(coarse, pl.ds(0, size, stride=pitch), begin)
    put(coarse, pl.ds(breadth - 1, size, stride=pitch), end)
    put(coarse, pl.ds(breadth, size, stride=pitch), right)

    def outside(row):
        return (top & (row == 0)) | (bottom & (row == rows - 1))

    slot = lax.broadcasted_iota(jnp.int32, (breadth, width), 0)
    ends = rightmost & (slot == breadth - 1)
    for t in range(frames):
        for r in range(rows):
            at = (t * tall + r) * pitch
            lost = top if r == 0 else bottom if r == rows - 1 else None
            for dj in range(2):
                value = jnp.maximum(take(coarse, slice(at + dj, at + dj + breadth)), 0.0)
                gone = [g for g in (lost, ends if dj else None) if g is not None]
                if gone:
                    value = jnp.where(functools.reduce(jnp.logical_or, gone), 0.0, value)
                near[dj, t, r] = value.astype(BF)
    row = lax.broadcasted_iota(jnp.int32, (size, width), 0) % tall
    far[0, :size] = jnp.where(outside(row) | leftmost, 0.0, jnp.maximum(left, 0.0))
    far[1, :size] = jnp.where(outside(row), 0.0, jnp.maximum(begin, 0.0))

    corners, later = rows - 1, frames - 2
    short = later * tall
    taps = [
        jnp.concatenate([
            near[dj, a : a + later, di : di + corners].reshape(-1, width),
            far[dj, a * tall + di : a * tall + di + short].astype(BF),
        ], 0)
        for a in range(3) for di in range(2) for dj in range(2)
    ]
    found = jnp.dot(
        jnp.concatenate(taps, 1), summed[...].reshape(-1, summed.shape[-1]), preferred_element_type=F32
    )
    found = jnp.maximum(found, 0.0)
    full = later * corners * breadth
    half = found.shape[1] // 2
    for t in range(later):
        for i in range(corners):
            at, to = (t * corners + i) * breadth, (t * tall + i) * pitch + SLACK
            put(grown, slice(to, to + breadth), found[at : at + breadth])
    put(grown, pl.ds(SLACK - 1, short, stride=pitch), found[full:])
    slot = lax.broadcasted_iota(jnp.int32, (breadth, half), 0)
    side = lax.broadcasted_iota(jnp.int32, (breadth, half), 1) < half // 2
    begins = leftmost & (slot == 0) & side
    ends = rightmost & (slot == breadth - 1) & ~side
    for t in range(later):
        for i in range(corners):
            for py in range(2):
                blocks = range(py * half // LANES, (py + 1) * half // LANES)
                lost = (top if py == 0 and i == 0 else bottom if py == 1 and i == corners - 1 else None)
                for dj, gone in enumerate((begins, ends)):
                    gone = gone if lost is None else gone | lost
                    at = (t * tall + i) * pitch + SLACK - 1 + dj
                    value = take(grown, slice(at, at + breadth), blocks)
                    fine[dj, 2 * i + py, t] = jnp.where(gone, 0.0, value).astype(BF)

    high, kept, wide = 2 * corners - 2, later - 2, out.shape[-1]
    taps = [
        fine[dj, b : b + high, a : a + kept].reshape(-1, half)
        for a in range(3) for b in range(3) for dj in range(2)
    ]
    found = jnp.dot(
        jnp.concatenate(taps, 1), paired[...].reshape(-1, paired.shape[-1]), preferred_element_type=F32
    )
    for y in range(high):
        for t in range(kept):
            at = (y * kept + t) * breadth
            for q in range(2):
                spread[t, y, pl.ds(q, breadth, stride=2), :] = found[
                    at : at + breadth, q * wide : (q + 1) * wide
                ]
    out[...] = spread[...].astype(BF)


def per_device(latent, w_first, w_second, w_third):
    frames, height, breadth, width = latent.shape
    mid, fine = w_first.shape[-1], w_second.shape[-1]
    last = w_third.shape[-1]
    sections = lax.axis_size("section")
    pieces, got, left, by = [], [], EARLIER, 1
    while left > 0:
        take = min(left, frames)
        ring = [(i, (i + by) % sections) for i in range(sections)]
        got.insert(0, lax.ppermute(latent[frames - take :], "section", ring))
        pieces.insert(0, (take, by))
        left, by = left - take, by + 1
    summed, paired, ready = call(
        kernels,
        [((3, 2, 2, mid, 4 * fine), BF), ((3, 3, 2, 2 * fine, 2 * last), BF), ((8, LANES), F32)],
        [w_second, w_third], flops=COVER, name="kernels",
    )
    total = frames + EARLIER
    row_places, col_places = lax.axis_size("row"), lax.axis_size("col")
    rounds, cols = len(swaps(row_places)), len(swaps(col_places))
    whole = row_places == 2 and cols == 2 and height == 2 * RIM
    payload = [] if whole else [((total, RIM, breadth, width), BF)] * rounds
    field, *sends = call(
        functools.partial(join_frames, pieces=pieces),
        [((total, height, breadth, width), BF)] + payload,
        [latent, ready, *got], flops=COVER, name="join_frames",
    )
    rows_got = exchange([field] if whole else sends, "row")
    tall = height + 2 * RIM
    sides = [((RIM, total * tall, width), BF)] * (1 if whole else cols)
    *sends, own = call(
        functools.partial(strips, rows=rounds, whole=whole),
        sides + [((2 * RIM, total * tall, width), BF)], [field, *rows_got],
        [(blocked(total * tall * breadth, width), F32)], name="strips",
    )
    early = total - 2

    def inner(begin, count, *after):
        return call(
            functools.partial(first_inner, rows=rounds, whole=whole, begin=begin),
            [((count, tall - 2, breadth, mid), F32)], [field, *rows_got, w_first, *after],
            [((3, count + 2, tall, breadth, width), BF)],
            flops=2 * 27 * count * (tall - 2) * breadth * width * mid, name="first_inner",
        )

    if whole:
        pairs = [
            (core * col_places + i, core * col_places + j)
            for core, pairing in enumerate(swaps(col_places)) for i, j in pairing
        ]
        came = lax.ppermute(sends[0], ("row", "col"), pairs)
        cut = 5 * early // 8
        inners = inner(0, cut)
        cols_got = [came, *exchange([came], "row")]
        inners += inner(cut, early - cut, came)
    else:
        cols_got = exchange(sends, "col")
        inners = inner(0, early)
    later, corners = early - 2, tall - 3
    size = early * tall
    (out,) = call(
        functools.partial(rest, cols=cols, parts=len(inners), whole=whole),
        [((frames, 2 * height, 2 * breadth, last), BF)],
        [*inners, own, *cols_got, w_first, summed, paired],
        [
            ((4 * RIM, total * tall, width), BF),
            (blocked(size * (breadth + SLACK), mid), F32),
            ((2, early, tall - 2, breadth, mid), BF),
            ((2, size + 8, mid), F32),
            (blocked(later * tall * (breadth + SLACK), 4 * fine), F32),
            ((2, 2 * corners, later, breadth, 2 * fine), BF),
            ((frames, 2 * height, 2 * breadth, last), F32),
        ],
        flops=4 * 10**9, name="rest",
    )
    return out


def solution(mesh):
    in_specs = (P("section", "row", "col", None), P(), P(), P())
    out_specs = P("section", "row", "col", None)
    return jax.shard_map(
        per_device, mesh=mesh, in_specs=in_specs, out_specs=out_specs, check_vma=False
    )
```

```python
import functools

import jax
import jax.numpy as jnp
from jax import lax
from jax.experimental import pallas as pl
from jax.experimental.pallas import tpu as pltpu
from jax.sharding import PartitionSpec as P

BF, F32 = jnp.bfloat16, jnp.float32
EARLIER = 6
RIM = 2


def call(body, outs, args, scratch=(), flops=0, name=None):
    spec = pl.BlockSpec(memory_space=pltpu.VMEM)
    outs = [jax.ShapeDtypeStruct(shape, kind) for shape, kind in outs]
    size = sum(a.size * a.dtype.itemsize for a in [*args, *outs])
    return pl.pallas_call(
        body, out_shape=outs, in_specs=[spec] * len(args), out_specs=[spec] * len(outs),
        scratch_shapes=[pltpu.VMEM(*s) for s in scratch], name=name,
        cost_estimate=pl.CostEstimate(flops=flops, bytes_accessed=size, transcendentals=0),
        compiler_params=pltpu.CompilerParams(vmem_limit_bytes=32 << 20),
    )(*args)


LANES = 128
COVER = 4 * 10**9
SLACK = 8


def put(ref, rows, value):
    for k in range(ref.shape[0]):
        ref[k, rows, :] = value[:, k * LANES : (k + 1) * LANES]


def take(ref, rows, blocks=None):
    blocks = range(ref.shape[0]) if blocks is None else blocks
    return jnp.concatenate([ref[k, rows, :] for k in blocks], 1)


def blocked(rows, width):
    return (width // LANES, rows, LANES)


def swaps(size):
    assert size % 2 == 0
    rounds = [[(i, i + 1) for i in range(0, size, 2)]]
    if size > 2:
        rounds.append([(i, (i + 1) % size) for i in range(1, size, 2)])
    return [pairs + [(j, i) for i, j in pairs] for pairs in rounds]


def exchange(sends, axis):
    return [lax.ppermute(s, axis, pairs) for s, pairs in zip(sends, swaps(lax.axis_size(axis)))]


def arrived(axis, got):
    place, size = lax.axis_index(axis), lax.axis_size(axis)
    even = place % 2 == 0
    if len(got) == 1:
        before = after = got[0]
    else:
        before, after = jnp.where(even, got[1], got[0]), jnp.where(even, got[0], got[1])
    zero = jnp.zeros_like(before)
    return jnp.where(place > 0, before, zero), jnp.where(place < size - 1, after, zero)


def join_frames(*refs, pieces):
    own, got = refs[0], refs[2 : 2 + len(pieces)]
    field, sends = refs[2 + len(pieces)], refs[3 + len(pieces) :]
    place, at = lax.axis_index("section"), 0
    for (take, by), ref in zip(pieces, got):
        field[at : at + take] = jnp.where(place >= by, ref[...], jnp.zeros_like(ref))
        at += take
    field[at:] = own[...]
    even = lax.axis_index("row") % 2 == 0
    last = field.shape[1] - RIM
    for k in range(len(sends)):
        start = jnp.where(even, 0, last) if k else jnp.where(even, last, 0)
        sends[k][...] = field[:, pl.ds(start, RIM)]


def rims(field, got, whole):
    if whole:
        got = [jnp.where(lax.axis_index("row") == 0, got[0][:, :RIM], got[0][:, -RIM:])]
    else:
        got = [g[...] for g in got]
    return arrived("row", got)


def strips(*refs, rows, whole):
    field, got = refs[0], refs[1 : 1 + rows]
    sends, own, wide = refs[1 + rows : -2], refs[-2], refs[-1]
    frames, height, breadth, width = field.shape
    if whole:
        upper = lax.axis_index("row") == 0
    else:
        before, after = rims(field, got, whole)
    size = wide.shape[1] // frames
    tall = size // breadth
    for t in range(frames):
        if whole:
            a, b = field[t].astype(F32), got[0][t].astype(F32)
            rows_of = [jnp.where(upper, a, b), jnp.where(upper, b, a)]
        else:
            rows_of = [before[t].astype(F32), field[t].astype(F32), after[t].astype(F32)]
        put(wide, slice(t * size, (t + 1) * size), jnp.concatenate(rows_of, 0).reshape(size, width))
    for i, c in enumerate([0, 1, breadth - 2, breadth - 1]):
        own[i] = take(wide, pl.ds(c, frames * tall, stride=breadth)).astype(BF)
    right = lax.axis_index("col") % 2 == 0
    if whole:
        right = right == (lax.axis_index("row") == 0)
    for k, send in enumerate(sends):
        start = jnp.where(right, 0, RIM) if k else jnp.where(right, RIM, 0)
        send[...] = own[pl.ds(start, RIM)]


def first_inner(*refs, rows, whole, begin):
    field, got, kernel = refs[0], refs[1 : 1 + rows], refs[1 + rows]
    out, wide = refs[-2:]
    count = out.shape[0]
    _, height, breadth, width = field.shape
    before, after = rims(field, got, whole)
    tall = height + 2 * RIM
    size = tall * breadth
    col = lax.broadcasted_iota(jnp.int32, (size, width), 0) % breadth
    for t in range(count + 2):
        rows_of = jnp.concatenate([before[begin + t], field[begin + t], after[begin + t]], 0)
        wide[1, t] = rows_of
        flat = rows_of.reshape(size, width).astype(F32)
        lower = jnp.where(col == 0, 0.0, pltpu.roll(flat, 1, 0))
        upper = jnp.where(col == breadth - 1, 0.0, pltpu.roll(flat, size - 1, 0))
        wide[0, t] = lower.astype(BF).reshape(rows_of.shape)
        wide[2, t] = upper.astype(BF).reshape(rows_of.shape)
    taps = [
        wide[e, a : a + count, b : b + tall - 2].reshape(-1, width)
        for a in range(3) for b in range(3) for e in range(3)
    ]
    found = jnp.dot(
        jnp.concatenate(taps, 1), kernel[...].reshape(-1, kernel.shape[-1]), preferred_element_type=F32
    )
    out[...] = found.reshape(out.shape)


def kernels(second, third, summed, paired, ready):
    ready[...] = jnp.zeros_like(ready)
    fine = second.shape[-1]
    reads = [[(0, 1), (2,)], [(0,), (1, 2)]]
    for a in range(3):
        tap = [[second[a, b, e].astype(F32) for e in range(3)] for b in range(3)]
        for di in range(2):
            for dj in range(2):
                for py in range(2):
                    for px in range(2):
                        parts = [tap[b][e] for b in reads[py][di] for e in reads[px][dj]]
                        at = (2 * py + px) * fine
                        summed[a, di, dj, :, at : at + fine] = sum(parts[1:], parts[0]).astype(BF)
    width, out = third.shape[-2:]
    for a in range(3):
        for b in range(3):
            for dj in range(2):
                for px in range(2):
                    for q in range(2):
                        e = 2 * dj + px - q
                        block = third[a, b, e] if 0 <= e < 3 else jnp.zeros((width, out), BF)
                        paired[a, b, dj, px * width : (px + 1) * width, q * out : (q + 1) * out] = block


def limits(axis):
    return lax.axis_index(axis) == 0, lax.axis_index(axis) == lax.axis_size(axis) - 1


def first_outer(*refs, cols, parts, whole):
    inner, own, got = refs[:parts], refs[parts], refs[parts + 1 : parts + 1 + cols]
    kernel, near, far, edge, coarse = refs[parts + 1 + cols :]
    rows, breadth, width = inner[0].shape[1:]
    frames = sum(part.shape[0] for part in inner)
    tall = rows + 2
    (top, bottom), (leftmost, rightmost) = limits("row"), limits("col")

    got = [g[...] for g in got]
    if whole:
        got = [jnp.where(top, *got), jnp.where(top, *got[::-1])]
    before, after = arrived("col", got)
    size = frames * tall
    for i in range(RIM):
        edge[i], edge[RIM + i] = before[i], own[i]
        edge[2 * RIM + i], edge[3 * RIM + i] = own[RIM + i], after[i]
    lhs = jnp.concatenate([
        jnp.concatenate(
            [edge[i + e, a * tall : a * tall + size] for i in (0, 1, 4, 5)], 0
        )
        for a in range(3) for e in range(3)
    ], 1)
    rhs = jnp.concatenate([
        jnp.concatenate([kernel[a, b, e] for b in range(3)], 1) for a in range(3) for e in range(3)
    ], 0)
    found = jnp.dot(lhs, rhs, preferred_element_type=F32)
    row = lax.broadcasted_iota(jnp.int32, (size, width), 0) % tall

    def placed(i):
        total = 0.0
        for b in range(3):
            value = found[i * size : (i + 1) * size, b * width : (b + 1) * width]
            if whole:
                shift = jnp.where(top, -RIM, tall // 2 - RIM) + b
                value = pltpu.roll(value, jnp.where(shift > 0, size - shift, -shift), 0)
                value = jnp.where((row + shift >= 0) & (row + shift < tall), value, 0.0)
            elif b:
                value = pltpu.roll(value, size - b, 0)
            total = total + value
        return total

    left, begin, end, right = [placed(i) for i in range(4)]

    pitch = breadth + SLACK
    at = 0
    for part in inner:
        for t in range(part.shape[0]):
            for r in range(rows):
                put(coarse, slice(at + r * pitch, at + r * pitch + breadth), part[t, r])
            at += tall * pitch
    put(coarse, pl.ds(0, size, stride=pitch), begin)
    put(coarse, pl.ds(breadth - 1, size, stride=pitch), end)
    put(coarse, pl.ds(breadth, size, stride=pitch), right)

    def outside(row):
        return (top & (row == 0)) | (bottom & (row == rows - 1))

    slot = lax.broadcasted_iota(jnp.int32, (breadth, width), 0)
    ends = rightmost & (slot == breadth - 1)
    for t in range(frames):
        for r in range(rows):
            at = (t * tall + r) * pitch
            lost = top if r == 0 else bottom if r == rows - 1 else None
            for dj in range(2):
                value = jnp.maximum(take(coarse, slice(at + dj, at + dj + breadth)), 0.0)
                gone = [g for g in (lost, ends if dj else None) if g is not None]
                if gone:
                    value = jnp.where(functools.reduce(jnp.logical_or, gone), 0.0, value)
                near[dj, t, r] = value.astype(BF)
    row = lax.broadcasted_iota(jnp.int32, (size, width), 0) % tall
    far[0, :size] = jnp.where(outside(row) | leftmost, 0.0, jnp.maximum(left, 0.0))
    far[1, :size] = jnp.where(outside(row), 0.0, jnp.maximum(begin, 0.0))


def second_conv(near, far, summed, fine, grown):
    _, frames, rows, breadth, width = near.shape
    tall, pitch = rows + 2, breadth + SLACK
    (top, bottom), (leftmost, rightmost) = limits("row"), limits("col")
    corners, later = rows - 1, frames - 2
    short = later * tall
    taps = [
        jnp.concatenate([
            near[dj, a : a + later, di : di + corners].reshape(-1, width),
            far[dj, a * tall + di : a * tall + di + short].astype(BF),
        ], 0)
        for a in range(3) for di in range(2) for dj in range(2)
    ]
    found = jnp.dot(
        jnp.concatenate(taps, 1), summed[...].reshape(-1, summed.shape[-1]), preferred_element_type=F32
    )
    found = jnp.maximum(found, 0.0)
    full = later * corners * breadth
    half = found.shape[1] // 2
    for t in range(later):
        for i in range(corners):
            at, to = (t * corners + i) * breadth, (t * tall + i) * pitch + SLACK
            put(grown, slice(to, to + breadth), found[at : at + breadth])
    put(grown, pl.ds(SLACK - 1, short, stride=pitch), found[full:])
    slot = lax.broadcasted_iota(jnp.int32, (breadth, half), 0)
    side = lax.broadcasted_iota(jnp.int32, (breadth, half), 1) < half // 2
    begins = leftmost & (slot == 0) & side
    ends = rightmost & (slot == breadth - 1) & ~side
    for t in range(later):
        for i in range(corners):
            for py in range(2):
                blocks = range(py * half // LANES, (py + 1) * half // LANES)
                lost = (top if py == 0 and i == 0 else bottom if py == 1 and i == corners - 1 else None)
                for dj, gone in enumerate((begins, ends)):
                    gone = gone if lost is None else gone | lost
                    at = (t * tall + i) * pitch + SLACK - 1 + dj
                    value = take(grown, slice(at, at + breadth), blocks)
                    fine[dj, 2 * i + py, t] = jnp.where(gone, 0.0, value).astype(BF)


def third_conv(fine, paired, out, spread):
    _, high, later, breadth, half = fine.shape
    high, kept, wide = high - 2, later - 2, out.shape[-1]
    taps = [
        fine[dj, b : b + high, a : a + kept].reshape(-1, half)
        for a in range(3) for b in range(3) for dj in range(2)
    ]
    found = jnp.dot(
        jnp.concatenate(taps, 1), paired[...].reshape(-1, paired.shape[-1]), preferred_element_type=F32
    )
    for y in range(high):
        for t in range(kept):
            at = (y * kept + t) * breadth
            for q in range(2):
                spread[t, y, pl.ds(q, breadth, stride=2), :] = found[
                    at : at + breadth, q * wide : (q + 1) * wide
                ]
    out[...] = spread[...].astype(BF)


def per_device(latent, w_first, w_second, w_third):
    frames, height, breadth, width = latent.shape
    mid, fine = w_first.shape[-1], w_second.shape[-1]
    last = w_third.shape[-1]
    sections = lax.axis_size("section")
    pieces, got, left, by = [], [], EARLIER, 1
    while left > 0:
        take = min(left, frames)
        ring = [(i, (i + by) % sections) for i in range(sections)]
        got.insert(0, lax.ppermute(latent[frames - take :], "section", ring))
        pieces.insert(0, (take, by))
        left, by = left - take, by + 1
    summed, paired, ready = call(
        kernels,
        [((3, 2, 2, mid, 4 * fine), BF), ((3, 3, 2, 2 * fine, 2 * last), BF), ((8, LANES), F32)],
        [w_second, w_third], flops=COVER, name="kernels",
    )
    total = frames + EARLIER
    row_places, col_places = lax.axis_size("row"), lax.axis_size("col")
    rounds, cols = len(swaps(row_places)), len(swaps(col_places))
    whole = row_places == 2 and cols == 2 and height == 2 * RIM
    payload = [] if whole else [((total, RIM, breadth, width), BF)] * rounds
    field, *sends = call(
        functools.partial(join_frames, pieces=pieces),
        [((total, height, breadth, width), BF)] + payload,
        [latent, ready, *got], flops=COVER, name="join_frames",
    )
    rows_got = exchange([field] if whole else sends, "row")
    tall = height + 2 * RIM
    sides = [((RIM, total * tall, width), BF)] * (1 if whole else cols)
    *sends, own = call(
        functools.partial(strips, rows=rounds, whole=whole),
        sides + [((2 * RIM, total * tall, width), BF)], [field, *rows_got],
        [(blocked(total * tall * breadth, width), F32)], name="strips",
    )
    early = total - 2

    def inner(begin, count, *after):
        return call(
            functools.partial(first_inner, rows=rounds, whole=whole, begin=begin),
            [((count, tall - 2, breadth, mid), F32)], [field, *rows_got, w_first, *after],
            [((3, count + 2, tall, breadth, width), BF)],
            flops=2 * 27 * count * (tall - 2) * breadth * width * mid, name="first_inner",
        )

    if whole:
        pairs = [
            (core * col_places + i, core * col_places + j)
            for core, pairing in enumerate(swaps(col_places)) for i, j in pairing
        ]
        came = lax.ppermute(sends[0], ("row", "col"), pairs)
        cut = 5 * early // 8
        inners = inner(0, cut)
        cols_got = [came, *exchange([came], "row")]
        inners += inner(cut, early - cut, came)
    else:
        cols_got = exchange(sends, "col")
        inners = inner(0, early)
    later, corners = early - 2, tall - 3
    size = early * tall
    near, far = call(
        functools.partial(first_outer, cols=cols, parts=len(inners), whole=whole),
        [((2, early, tall - 2, breadth, mid), BF), ((2, size + 8, mid), F32)],
        [*inners, own, *cols_got, w_first],
        [((4 * RIM, total * tall, width), BF), (blocked(size * (breadth + SLACK), mid), F32)],
        flops=10**9, name="first_outer",
    )
    (second,) = call(
        second_conv, [((2, 2 * corners, later, breadth, 2 * fine), BF)], [near, far, summed],
        [(blocked(later * tall * (breadth + SLACK), 4 * fine), F32)],
        flops=2 * 10**9, name="second_conv",
    )
    (out,) = call(
        third_conv, [((frames, 2 * height, 2 * breadth, last), BF)], [second, paired],
        [((frames, 2 * height, 2 * breadth, last), F32)], flops=10**9, name="third_conv",
    )
    return out


def solution(mesh):
    in_specs = (P("section", "row", "col", None), P(), P(), P())
    out_specs = P("section", "row", "col", None)
    return jax.shard_map(
        per_device, mesh=mesh, in_specs=in_specs, out_specs=out_specs, check_vma=False
    )
```

```python
import functools

import jax
import jax.numpy as jnp
from jax import lax
from jax.experimental import pallas as pl
from jax.experimental.pallas import tpu as pltpu
from jax.sharding import PartitionSpec as P

BF, F32 = jnp.bfloat16, jnp.float32
EARLIER = 6
RIM = 2


def call(body, outs, args, scratch=(), flops=0, name=None, to=pltpu.VMEM):
    spec = pl.BlockSpec(memory_space=pltpu.VMEM)
    outs = [jax.ShapeDtypeStruct(shape, kind) for shape, kind in outs]
    size = sum(a.size * a.dtype.itemsize for a in [*args, *outs])
    return pl.pallas_call(
        body, out_shape=outs, in_specs=[spec] * len(args),
        out_specs=[pl.BlockSpec(memory_space=to)] * len(outs), name=name,
        scratch_shapes=[pltpu.VMEM(*s) if isinstance(s, tuple) else s for s in scratch],
        cost_estimate=pl.CostEstimate(flops=flops, bytes_accessed=size, transcendentals=0),
        compiler_params=pltpu.CompilerParams(vmem_limit_bytes=32 << 20),
    )(*args)


LANES = 128
COVER = 4 * 10**9
SLACK = 8


def put(ref, rows, value):
    for k in range(ref.shape[0]):
        ref[k, rows, :] = value[:, k * LANES : (k + 1) * LANES]


def take(ref, rows, blocks=None):
    blocks = range(ref.shape[0]) if blocks is None else blocks
    return jnp.concatenate([ref[k, rows, :] for k in blocks], 1)


def blocked(rows, width):
    return (width // LANES, rows, LANES)


def swaps(size):
    assert size % 2 == 0
    rounds = [[(i, i + 1) for i in range(0, size, 2)]]
    if size > 2:
        rounds.append([(i, (i + 1) % size) for i in range(1, size, 2)])
    return [pairs + [(j, i) for i, j in pairs] for pairs in rounds]


def exchange(sends, axis):
    return [lax.ppermute(s, axis, pairs) for s, pairs in zip(sends, swaps(lax.axis_size(axis)))]


def arrived(axis, got):
    place, size = lax.axis_index(axis), lax.axis_size(axis)
    even = place % 2 == 0
    if len(got) == 1:
        before = after = got[0]
    else:
        before, after = jnp.where(even, got[1], got[0]), jnp.where(even, got[0], got[1])
    zero = jnp.zeros_like(before)
    return jnp.where(place > 0, before, zero), jnp.where(place < size - 1, after, zero)


def join_frames(*refs, pieces):
    own, got = refs[0], refs[2 : 2 + len(pieces)]
    field, sends = refs[2 + len(pieces)], refs[3 + len(pieces) :]
    place, at = lax.axis_index("section"), 0
    for (take, by), ref in zip(pieces, got):
        field[at : at + take] = jnp.where(place >= by, ref[...], jnp.zeros_like(ref))
        at += take
    field[at:] = own[...]
    even = lax.axis_index("row") % 2 == 0
    last = field.shape[1] - RIM
    for k in range(len(sends)):
        start = jnp.where(even, 0, last) if k else jnp.where(even, last, 0)
        sends[k][...] = field[:, pl.ds(start, RIM)]


def rims(field, got, whole):
    if whole:
        got = [jnp.where(lax.axis_index("row") == 0, got[0][:, :RIM], got[0][:, -RIM:])]
    else:
        got = [g[...] for g in got]
    return arrived("row", got)


def strips(*refs, rows, whole):
    field, got = refs[0], refs[1 : 1 + rows]
    sends, own, wide = refs[1 + rows : -2], refs[-2], refs[-1]
    frames, height, breadth, width = field.shape
    if whole:
        upper = lax.axis_index("row") == 0
    else:
        before, after = rims(field, got, whole)
    size = wide.shape[1] // frames
    tall = size // breadth
    for t in range(frames):
        if whole:
            a, b = field[t].astype(F32), got[0][t].astype(F32)
            rows_of = [jnp.where(upper, a, b), jnp.where(upper, b, a)]
        else:
            rows_of = [before[t].astype(F32), field[t].astype(F32), after[t].astype(F32)]
        put(wide, slice(t * size, (t + 1) * size), jnp.concatenate(rows_of, 0).reshape(size, width))
    for i, c in enumerate([0, 1, breadth - 2, breadth - 1]):
        own[i] = take(wide, pl.ds(c, frames * tall, stride=breadth)).astype(BF)
    right = lax.axis_index("col") % 2 == 0
    if whole:
        right = right == (lax.axis_index("row") == 0)
    for k, send in enumerate(sends):
        start = jnp.where(right, 0, RIM) if k else jnp.where(right, RIM, 0)
        send[...] = own[pl.ds(start, RIM)]


def first_inner(*refs, rows, whole, begin):
    field, got, kernel = refs[0], refs[1 : 1 + rows], refs[1 + rows]
    out, wide = refs[-2:]
    count = out.shape[0]
    _, height, breadth, width = field.shape
    before, after = rims(field, got, whole)
    tall = height + 2 * RIM
    size = tall * breadth
    col = lax.broadcasted_iota(jnp.int32, (size, width), 0) % breadth
    for t in range(count + 2):
        rows_of = jnp.concatenate([before[begin + t], field[begin + t], after[begin + t]], 0)
        wide[1, t] = rows_of
        flat = rows_of.reshape(size, width).astype(F32)
        lower = jnp.where(col == 0, 0.0, pltpu.roll(flat, 1, 0))
        upper = jnp.where(col == breadth - 1, 0.0, pltpu.roll(flat, size - 1, 0))
        wide[0, t] = lower.astype(BF).reshape(rows_of.shape)
        wide[2, t] = upper.astype(BF).reshape(rows_of.shape)
    taps = [
        wide[e, a : a + count, b : b + tall - 2].reshape(-1, width)
        for a in range(3) for b in range(3) for e in range(3)
    ]
    found = jnp.dot(
        jnp.concatenate(taps, 1), kernel[...].reshape(-1, kernel.shape[-1]), preferred_element_type=F32
    )
    out[...] = found.reshape(out.shape)


def kernels(second, third, summed, paired, ready):
    ready[...] = jnp.zeros_like(ready)
    fine = second.shape[-1]
    reads = [[(0, 1), (2,)], [(0,), (1, 2)]]
    for a in range(3):
        tap = [[second[a, b, e].astype(F32) for e in range(3)] for b in range(3)]
        for di in range(2):
            for dj in range(2):
                for py in range(2):
                    for px in range(2):
                        parts = [tap[b][e] for b in reads[py][di] for e in reads[px][dj]]
                        at = (2 * py + px) * fine
                        summed[a, di, dj, :, at : at + fine] = sum(parts[1:], parts[0]).astype(BF)
    width, out = third.shape[-2:]
    for a in range(3):
        for b in range(3):
            for dj in range(2):
                for px in range(2):
                    for q in range(2):
                        e = 2 * dj + px - q
                        block = third[a, b, e] if 0 <= e < 3 else jnp.zeros((width, out), BF)
                        paired[a, b, dj, px * width : (px + 1) * width, q * out : (q + 1) * out] = block


def limits(axis):
    return lax.axis_index(axis) == 0, lax.axis_index(axis) == lax.axis_size(axis) - 1


def first_outer(*refs, cols, parts, whole):
    inner, own, got = refs[:parts], refs[parts], refs[parts + 1 : parts + 1 + cols]
    kernel, near, far, edge, coarse = refs[parts + 1 + cols :]
    rows, breadth, width = inner[0].shape[1:]
    frames = sum(part.shape[0] for part in inner)
    tall = rows + 2
    (top, bottom), (leftmost, rightmost) = limits("row"), limits("col")

    got = [g[...] for g in got]
    if whole:
        got = [jnp.where(top, *got), jnp.where(top, *got[::-1])]
    before, after = arrived("col", got)
    size = frames * tall
    for i in range(RIM):
        edge[i], edge[RIM + i] = before[i], own[i]
        edge[2 * RIM + i], edge[3 * RIM + i] = own[RIM + i], after[i]
    lhs = jnp.concatenate([
        jnp.concatenate(
            [edge[i + e, a * tall : a * tall + size] for i in (0, 1, 4, 5)], 0
        )
        for a in range(3) for e in range(3)
    ], 1)
    rhs = jnp.concatenate([
        jnp.concatenate([kernel[a, b, e] for b in range(3)], 1) for a in range(3) for e in range(3)
    ], 0)
    found = jnp.dot(lhs, rhs, preferred_element_type=F32)
    row = lax.broadcasted_iota(jnp.int32, (size, width), 0) % tall

    def placed(i):
        total = 0.0
        for b in range(3):
            value = found[i * size : (i + 1) * size, b * width : (b + 1) * width]
            if whole:
                shift = jnp.where(top, -RIM, tall // 2 - RIM) + b
                value = pltpu.roll(value, jnp.where(shift > 0, size - shift, -shift), 0)
                value = jnp.where((row + shift >= 0) & (row + shift < tall), value, 0.0)
            elif b:
                value = pltpu.roll(value, size - b, 0)
            total = total + value
        return total

    left, begin, end, right = [placed(i) for i in range(4)]

    pitch = breadth + SLACK
    at = 0
    for part in inner:
        for t in range(part.shape[0]):
            for r in range(rows):
                put(coarse, slice(at + r * pitch, at + r * pitch + breadth), part[t, r])
            at += tall * pitch
    put(coarse, pl.ds(0, size, stride=pitch), begin)
    put(coarse, pl.ds(breadth - 1, size, stride=pitch), end)
    put(coarse, pl.ds(breadth, size, stride=pitch), right)

    def outside(row):
        return (top & (row == 0)) | (bottom & (row == rows - 1))

    slot = lax.broadcasted_iota(jnp.int32, (breadth, width), 0)
    ends = rightmost & (slot == breadth - 1)
    for t in range(frames):
        for r in range(rows):
            at = (t * tall + r) * pitch
            lost = top if r == 0 else bottom if r == rows - 1 else None
            for dj in range(2):
                value = jnp.maximum(take(coarse, slice(at + dj, at + dj + breadth)), 0.0)
                gone = [g for g in (lost, ends if dj else None) if g is not None]
                if gone:
                    value = jnp.where(functools.reduce(jnp.logical_or, gone), 0.0, value)
                near[dj, t, r] = value.astype(BF)
    row = lax.broadcasted_iota(jnp.int32, (size, width), 0) % tall
    far[0, :size] = jnp.where(outside(row) | leftmost, 0.0, jnp.maximum(left, 0.0))
    far[1, :size] = jnp.where(outside(row), 0.0, jnp.maximum(begin, 0.0))


def second_conv(near, far, summed, fine, grown):
    _, frames, rows, breadth, width = near.shape
    tall, pitch = rows + 2, breadth + SLACK
    (top, bottom), (leftmost, rightmost) = limits("row"), limits("col")
    corners, later = rows - 1, frames - 2
    short = later * tall
    taps = [
        jnp.concatenate([
            near[dj, a : a + later, di : di + corners].reshape(-1, width),
            far[dj, a * tall + di : a * tall + di + short].astype(BF),
        ], 0)
        for a in range(3) for di in range(2) for dj in range(2)
    ]
    found = jnp.dot(
        jnp.concatenate(taps, 1), summed[...].reshape(-1, summed.shape[-1]), preferred_element_type=F32
    )
    found = jnp.maximum(found, 0.0)
    full = later * corners * breadth
    half = found.shape[1] // 2
    for t in range(later):
        for i in range(corners):
            at, to = (t * corners + i) * breadth, (t * tall + i) * pitch + SLACK
            put(grown, slice(to, to + breadth), found[at : at + breadth])
    put(grown, pl.ds(SLACK - 1, short, stride=pitch), found[full:])
    slot = lax.broadcasted_iota(jnp.int32, (breadth, half), 0)
    side = lax.broadcasted_iota(jnp.int32, (breadth, half), 1) < half // 2
    begins = leftmost & (slot == 0) & side
    ends = rightmost & (slot == breadth - 1) & ~side
    for t in range(later):
        for i in range(corners):
            for py in range(2):
                blocks = range(py * half // LANES, (py + 1) * half // LANES)
                lost = (top if py == 0 and i == 0 else bottom if py == 1 and i == corners - 1 else None)
                for dj, gone in enumerate((begins, ends)):
                    gone = gone if lost is None else gone | lost
                    at = (t * tall + i) * pitch + SLACK - 1 + dj
                    value = take(grown, slice(at, at + breadth), blocks)
                    fine[dj, 2 * i + py, t] = jnp.where(gone, 0.0, value).astype(BF)


def third_conv(fine, paired, out, spread, ready, sems):
    _, high, later, breadth, half = fine.shape
    high, kept, wide = high - 2, later - 2, out.shape[-1]
    steps = sems.shape[0]
    count = kept // steps
    kernel = paired[...].reshape(-1, paired.shape[-1])

    def leave(step):
        mine = pl.ds(step * count, count)
        return pltpu.make_async_copy(ready.at[mine], out.at[mine], sems.at[step])

    @pl.loop(0, steps)
    def _(step):
        begin = step * count
        taps = [
            fine[dj, b : b + high, pl.ds(begin + a, count)].reshape(-1, half)
            for a in range(3) for b in range(3) for dj in range(2)
        ]
        found = jnp.dot(jnp.concatenate(taps, 1), kernel, preferred_element_type=F32)
        for y in range(high):
            for t in range(count):
                at = (y * count + t) * breadth
                for q in range(2):
                    spread[t, y, pl.ds(q, breadth, stride=2), :] = found[
                        at : at + breadth, q * wide : (q + 1) * wide
                    ]
        ready[pl.ds(begin, count)] = spread[...].astype(BF)
        leave(step).start()

    for step in range(steps):
        leave(step).wait()


def per_device(latent, w_first, w_second, w_third):
    frames, height, breadth, width = latent.shape
    mid, fine = w_first.shape[-1], w_second.shape[-1]
    last = w_third.shape[-1]
    sections = lax.axis_size("section")
    pieces, got, left, by = [], [], EARLIER, 1
    while left > 0:
        take = min(left, frames)
        ring = [(i, (i + by) % sections) for i in range(sections)]
        got.insert(0, lax.ppermute(latent[frames - take :], "section", ring))
        pieces.insert(0, (take, by))
        left, by = left - take, by + 1
    summed, paired, ready = call(
        kernels,
        [((3, 2, 2, mid, 4 * fine), BF), ((3, 3, 2, 2 * fine, 2 * last), BF), ((8, LANES), F32)],
        [w_second, w_third], flops=COVER, name="kernels",
    )
    total = frames + EARLIER
    row_places, col_places = lax.axis_size("row"), lax.axis_size("col")
    rounds, cols = len(swaps(row_places)), len(swaps(col_places))
    whole = row_places == 2 and cols == 2 and height == 2 * RIM
    payload = [] if whole else [((total, RIM, breadth, width), BF)] * rounds
    field, *sends = call(
        functools.partial(join_frames, pieces=pieces),
        [((total, height, breadth, width), BF)] + payload,
        [latent, ready, *got], flops=COVER, name="join_frames",
    )
    rows_got = exchange([field] if whole else sends, "row")
    tall = height + 2 * RIM
    sides = [((RIM, total * tall, width), BF)] * (1 if whole else cols)
    *sends, own = call(
        functools.partial(strips, rows=rounds, whole=whole),
        sides + [((2 * RIM, total * tall, width), BF)], [field, *rows_got],
        [(blocked(total * tall * breadth, width), F32)], name="strips",
    )
    early = total - 2

    def inner(begin, count, *after):
        return call(
            functools.partial(first_inner, rows=rounds, whole=whole, begin=begin),
            [((count, tall - 2, breadth, mid), F32)], [field, *rows_got, w_first, *after],
            [((3, count + 2, tall, breadth, width), BF)],
            flops=2 * 27 * count * (tall - 2) * breadth * width * mid, name="first_inner",
        )

    if whole:
        pairs = []
        for section in range(sections):
            for core, pairing in enumerate(swaps(col_places)):
                at = (section * row_places + core) * col_places
                for i, j in pairing:
                    if abs(i - j) > 1 and sections % 2 == 0:
                        to = ((section ^ 1) * row_places + core) * col_places
                        pairs.append((at + i, to + i))
                    else:
                        pairs.append((at + i, at + j))
        came = lax.ppermute(sends[0], ("section", "row", "col"), pairs)
        cut = 5 * early // 8
        inners = inner(0, cut)
        cols_got = [came, *exchange([came], "row")]
        inners += inner(cut, early - cut, came)
    else:
        cols_got = exchange(sends, "col")
        inners = inner(0, early)
    later, corners = early - 2, tall - 3
    size = early * tall
    near, far = call(
        functools.partial(first_outer, cols=cols, parts=len(inners), whole=whole),
        [((2, early, tall - 2, breadth, mid), BF), ((2, size + 8, mid), F32)],
        [*inners, own, *cols_got, w_first],
        [((4 * RIM, total * tall, width), BF), (blocked(size * (breadth + SLACK), mid), F32)],
        flops=10**9, name="first_outer",
    )
    (second,) = call(
        second_conv, [((2, 2 * corners, later, breadth, 2 * fine), BF)], [near, far, summed],
        [(blocked(later * tall * (breadth + SLACK), 4 * fine), F32)],
        flops=2 * 10**9, name="second_conv",
    )
    steps = 2 if frames % 2 == 0 else 1
    (out,) = call(
        third_conv, [((frames, 2 * height, 2 * breadth, last), BF)], [second, paired],
        [
            ((frames // steps, 2 * height, 2 * breadth, last), F32),
            ((frames, 2 * height, 2 * breadth, last), BF), pltpu.SemaphoreType.DMA((steps,)),
        ],
        flops=10**9, name="third_conv", to=pl.ANY,
    )
    return out


def solution(mesh):
    in_specs = (P("section", "row", "col", None), P(), P(), P())
    out_specs = P("section", "row", "col", None)
    return jax.shard_map(
        per_device, mesh=mesh, in_specs=in_specs, out_specs=out_specs, check_vma=False
    )
```

```python
import functools

import jax
import jax.numpy as jnp
from jax import lax
from jax.experimental import pallas as pl
from jax.experimental.pallas import tpu as pltpu
from jax.sharding import PartitionSpec as P


BF, F32 = jnp.bfloat16, jnp.float32
EARLIER = 6
RIM = 2


def call(body, outs, args, scratch=(), flops=0, to=pltpu.VMEM):
    spec = pl.BlockSpec(memory_space=pltpu.VMEM)
    outs = [jax.ShapeDtypeStruct(shape, kind) for shape, kind in outs]
    size = sum(a.size * a.dtype.itemsize for a in [*args, *outs])
    return pl.pallas_call(
        body, out_shape=outs, in_specs=[spec] * len(args),
        out_specs=[pl.BlockSpec(memory_space=to)] * len(outs),
        scratch_shapes=[pltpu.VMEM(*s) if isinstance(s, tuple) else s for s in scratch],
        cost_estimate=pl.CostEstimate(flops=flops, bytes_accessed=size, transcendentals=0),
        compiler_params=pltpu.CompilerParams(vmem_limit_bytes=32 << 20),
    )(*args)


LANES = 128
COVER = 4 * 10**9
SLACK = 8


def put(ref, rows, value):
    for k in range(ref.shape[0]):
        ref[k, rows, :] = value[:, k * LANES : (k + 1) * LANES]


def take(ref, rows, blocks=None):
    blocks = range(ref.shape[0]) if blocks is None else blocks
    return jnp.concatenate([ref[k, rows, :] for k in blocks], 1)


def blocked(rows, width):
    return (width // LANES, rows, LANES)


def swaps(size):
    assert size % 2 == 0
    rounds = [[(i, i + 1) for i in range(0, size, 2)]]
    if size > 2:
        rounds.append([(i, (i + 1) % size) for i in range(1, size, 2)])
    return [pairs + [(j, i) for i, j in pairs] for pairs in rounds]


def exchange(sends, axis):
    return [lax.ppermute(s, axis, pairs) for s, pairs in zip(sends, swaps(lax.axis_size(axis)))]


def arrived(axis, got):
    place, size = lax.axis_index(axis), lax.axis_size(axis)
    even = place % 2 == 0
    if len(got) == 1:
        before = after = got[0]
    else:
        before, after = jnp.where(even, got[1], got[0]), jnp.where(even, got[0], got[1])
    zero = jnp.zeros_like(before)
    return jnp.where(place > 0, before, zero), jnp.where(place < size - 1, after, zero)


def lead(out):
    out[...] = jnp.zeros_like(out)


def tails(latent, lead, *outs):
    for out in outs:
        out[...] = latent[latent.shape[0] - out.shape[0] :]


def join_frames(*refs, pieces):
    own, got = refs[0], refs[2 : 2 + len(pieces)]
    field, sends = refs[2 + len(pieces)], refs[3 + len(pieces) :]
    place, at = lax.axis_index("section"), 0
    for (take, by), ref in zip(pieces, got):
        field[at : at + take] = jnp.where(place >= by, ref[...], jnp.zeros_like(ref))
        at += take
    field[at:] = own[...]
    even = lax.axis_index("row") % 2 == 0
    last = field.shape[1] - RIM
    for k in range(len(sends)):
        start = jnp.where(even, 0, last) if k else jnp.where(even, last, 0)
        sends[k][...] = field[:, pl.ds(start, RIM)]


def rims(got, whole):
    if whole:
        got = [jnp.where(lax.axis_index("row") == 0, got[0][:, :RIM], got[0][:, -RIM:])]
    else:
        got = [g[...] for g in got]
    return arrived("row", got)


def strips(*refs, rows, whole):
    field, got = refs[0], refs[1 : 1 + rows]
    sends, own, wide = refs[1 + rows : -2], refs[-2], refs[-1]
    frames, _, breadth, width = field.shape
    if whole:
        upper = lax.axis_index("row") == 0
    else:
        before, after = rims(got, whole)
    size = wide.shape[1] // frames
    tall = size // breadth
    for t in range(frames):
        if whole:
            a, b = field[t].astype(F32), got[0][t].astype(F32)
            rows_of = [jnp.where(upper, a, b), jnp.where(upper, b, a)]
        else:
            rows_of = [before[t].astype(F32), field[t].astype(F32), after[t].astype(F32)]
        put(wide, slice(t * size, (t + 1) * size), jnp.concatenate(rows_of, 0).reshape(size, width))
    for i, c in enumerate([0, 1, breadth - 2, breadth - 1]):
        own[i] = take(wide, pl.ds(c, frames * tall, stride=breadth)).astype(BF)
    right = lax.axis_index("col") % 2 == 0
    if whole:
        right = right == (lax.axis_index("row") == 0)
    for k, send in enumerate(sends):
        start = jnp.where(right, 0, RIM) if k else jnp.where(right, RIM, 0)
        send[...] = own[pl.ds(start, RIM)]


def first_inner(*refs, rows, whole, begin):
    field, got, kernel = refs[0], refs[1 : 1 + rows], refs[1 + rows]
    out, wide = refs[-2:]
    count = out.shape[0]
    _, height, breadth, width = field.shape
    before, after = rims(got, whole)
    tall = height + 2 * RIM
    size = tall * breadth
    col = lax.broadcasted_iota(jnp.int32, (size, width), 0) % breadth
    for t in range(count + 2):
        rows_of = jnp.concatenate([before[begin + t], field[begin + t], after[begin + t]], 0)
        wide[1, t] = rows_of
        flat = rows_of.reshape(size, width).astype(F32)
        lower = jnp.where(col == 0, 0.0, pltpu.roll(flat, 1, 0))
        upper = jnp.where(col == breadth - 1, 0.0, pltpu.roll(flat, size - 1, 0))
        wide[0, t] = lower.astype(BF).reshape(rows_of.shape)
        wide[2, t] = upper.astype(BF).reshape(rows_of.shape)
    taps = [
        wide[e, a : a + count, b : b + tall - 2].reshape(-1, width)
        for a in range(3) for b in range(3) for e in range(3)
    ]
    found = jnp.dot(
        jnp.concatenate(taps, 1), kernel[...].reshape(-1, kernel.shape[-1]), preferred_element_type=F32
    )
    out[...] = found.reshape(out.shape)


def kernels(second, third, summed, paired, ready):
    ready[...] = jnp.zeros_like(ready)
    fine = second.shape[-1]
    reads = [[(0, 1), (2,)], [(0,), (1, 2)]]
    for a in range(3):
        tap = [[second[a, b, e].astype(F32) for e in range(3)] for b in range(3)]
        for di in range(2):
            for dj in range(2):
                for py in range(2):
                    for px in range(2):
                        parts = [tap[b][e] for b in reads[py][di] for e in reads[px][dj]]
                        at = (2 * py + px) * fine
                        summed[a, di, dj, :, at : at + fine] = sum(parts[1:], parts[0]).astype(BF)
    width, out = third.shape[-2:]
    for a in range(3):
        for b in range(3):
            for dj in range(2):
                for px in range(2):
                    for q in range(2):
                        e = 2 * dj + px - q
                        block = third[a, b, e] if 0 <= e < 3 else jnp.zeros((width, out), BF)
                        paired[a, b, dj, px * width : (px + 1) * width, q * out : (q + 1) * out] = block


def limits(axis):
    return lax.axis_index(axis) == 0, lax.axis_index(axis) == lax.axis_size(axis) - 1


def first_outer(*refs, cols, parts, whole):
    inner, own, got = refs[:parts], refs[parts], refs[parts + 1 : parts + 1 + cols]
    kernel, near, far, edge, coarse = refs[parts + 1 + cols :]
    rows, breadth, width = inner[0].shape[1:]
    frames = sum(part.shape[0] for part in inner)
    tall = rows + 2
    (top, bottom), (leftmost, rightmost) = limits("row"), limits("col")

    got = [g[...] for g in got]
    if whole:
        got = [jnp.where(top, *got), jnp.where(top, *got[::-1])]
    before, after = arrived("col", got)
    size = frames * tall
    for i in range(RIM):
        edge[i], edge[RIM + i] = before[i], own[i]
        edge[2 * RIM + i], edge[3 * RIM + i] = own[RIM + i], after[i]
    lhs = jnp.concatenate([
        jnp.concatenate(
            [edge[i + e, a * tall : a * tall + size] for i in (0, 1, 4, 5)], 0
        )
        for a in range(3) for e in range(3)
    ], 1)
    rhs = jnp.concatenate([
        jnp.concatenate([kernel[a, b, e] for b in range(3)], 1) for a in range(3) for e in range(3)
    ], 0)
    found = jnp.dot(lhs, rhs, preferred_element_type=F32)
    row = lax.broadcasted_iota(jnp.int32, (size, width), 0) % tall

    def placed(i):
        total = 0.0
        for b in range(3):
            value = found[i * size : (i + 1) * size, b * width : (b + 1) * width]
            if whole:
                shift = jnp.where(top, -RIM, tall // 2 - RIM) + b
                value = pltpu.roll(value, jnp.where(shift > 0, size - shift, -shift), 0)
                value = jnp.where((row + shift >= 0) & (row + shift < tall), value, 0.0)
            elif b:
                value = pltpu.roll(value, size - b, 0)
            total = total + value
        return total

    left, begin, end, right = [placed(i) for i in range(4)]

    pitch = breadth + SLACK
    at = 0
    for part in inner:
        for t in range(part.shape[0]):
            for r in range(rows):
                put(coarse, slice(at + r * pitch, at + r * pitch + breadth), part[t, r])
            at += tall * pitch
    put(coarse, pl.ds(0, size, stride=pitch), begin)
    put(coarse, pl.ds(breadth - 1, size, stride=pitch), end)
    put(coarse, pl.ds(breadth, size, stride=pitch), right)

    def outside(row):
        return (top & (row == 0)) | (bottom & (row == rows - 1))

    slot = lax.broadcasted_iota(jnp.int32, (breadth, width), 0)
    ends = rightmost & (slot == breadth - 1)
    for t in range(frames):
        for r in range(rows):
            at = (t * tall + r) * pitch
            lost = top if r == 0 else bottom if r == rows - 1 else None
            for dj in range(2):
                value = jnp.maximum(take(coarse, slice(at + dj, at + dj + breadth)), 0.0)
                gone = [g for g in (lost, ends if dj else None) if g is not None]
                if gone:
                    value = jnp.where(functools.reduce(jnp.logical_or, gone), 0.0, value)
                near[dj, t, r] = value.astype(BF)
    row = lax.broadcasted_iota(jnp.int32, (size, width), 0) % tall
    far[0, :size] = jnp.where(outside(row) | leftmost, 0.0, jnp.maximum(left, 0.0))
    far[1, :size] = jnp.where(outside(row), 0.0, jnp.maximum(begin, 0.0))


def second_conv(near, far, summed, fine, grown):
    _, frames, rows, breadth, width = near.shape
    tall, pitch = rows + 2, breadth + SLACK
    (top, bottom), (leftmost, rightmost) = limits("row"), limits("col")
    corners, later = rows - 1, frames - 2
    short = later * tall
    taps = [
        jnp.concatenate([
            near[dj, a : a + later, di : di + corners].reshape(-1, width),
            far[dj, a * tall + di : a * tall + di + short].astype(BF),
        ], 0)
        for a in range(3) for di in range(2) for dj in range(2)
    ]
    found = jnp.dot(
        jnp.concatenate(taps, 1), summed[...].reshape(-1, summed.shape[-1]), preferred_element_type=F32
    )
    found = jnp.maximum(found, 0.0)
    full = later * corners * breadth
    half = found.shape[1] // 2
    for t in range(later):
        for i in range(corners):
            at, to = (t * corners + i) * breadth, (t * tall + i) * pitch + SLACK
            put(grown, slice(to, to + breadth), found[at : at + breadth])
    put(grown, pl.ds(SLACK - 1, short, stride=pitch), found[full:])
    slot = lax.broadcasted_iota(jnp.int32, (breadth, half), 0)
    side = lax.broadcasted_iota(jnp.int32, (breadth, half), 1) < half // 2
    begins = leftmost & (slot == 0) & side
    ends = rightmost & (slot == breadth - 1) & ~side
    for t in range(later):
        for i in range(corners):
            for py in range(2):
                blocks = range(py * half // LANES, (py + 1) * half // LANES)
                lost = (top if py == 0 and i == 0 else bottom if py == 1 and i == corners - 1 else None)
                for dj, gone in enumerate((begins, ends)):
                    gone = gone if lost is None else gone | lost
                    at = (t * tall + i) * pitch + SLACK - 1 + dj
                    value = take(grown, slice(at, at + breadth), blocks)
                    fine[dj, 2 * i + py, t] = jnp.where(gone, 0.0, value).astype(BF)


def third_conv(fine, paired, out, spread, ready, sems):
    _, high, later, breadth, half = fine.shape
    high, kept, wide = high - 2, later - 2, out.shape[-1]
    steps = sems.shape[0]
    count = kept // steps

    def leave(step):
        mine = pl.ds(step * count, count)
        return pltpu.make_async_copy(ready.at[mine], out.at[mine], sems.at[step])

    @pl.loop(0, steps)
    def _(step):
        begin = step * count
        taps = [
            fine[dj, b : b + high, pl.ds(begin + a, count)].reshape(-1, half)
            for a in range(3) for b in range(3) for dj in range(2)
        ]
        kernel = paired[...].reshape(-1, paired.shape[-1])
        found = jnp.dot(jnp.concatenate(taps, 1), kernel, preferred_element_type=F32)
        for y in range(high):
            for t in range(count):
                at = (y * count + t) * breadth
                for q in range(2):
                    spread[t, y, pl.ds(q, breadth, stride=2), :] = found[
                        at : at + breadth, q * wide : (q + 1) * wide
                    ]
        ready[pl.ds(begin, count)] = spread[...].astype(BF)
        leave(step).start()

    for step in range(steps):
        leave(step).wait()


def per_device(latent, w_first, w_second, w_third):
    frames, height, breadth, width = latent.shape
    mid, fine = w_first.shape[-1], w_second.shape[-1]
    last = w_third.shape[-1]
    sections = lax.axis_size("section")
    pieces, left, by = [], EARLIER, 1
    while left > 0:
        pieces.insert(0, (min(left, frames), by))
        left, by = left - frames, by + 1
    (first_of_all,) = call(lead, [((8, LANES), F32)], [], flops=COVER)
    part = [take for take, _ in pieces if take < frames]
    if part:
        ends = list(call(
            tails, [((take, height, breadth, width), BF) for take in part],
            [latent, first_of_all],
        ))
    got = []
    for take, by in pieces:
        ring = [(i, (i + by) % sections) for i in range(sections)]
        got.append(lax.ppermute(ends.pop(0) if take < frames else latent, "section", ring))
    summed, paired, ready = call(
        kernels,
        [((3, 2, 2, mid, 4 * fine), BF), ((3, 3, 2, 2 * fine, 2 * last), BF), ((8, LANES), F32)],
        [w_second, w_third], flops=COVER,
    )
    total = frames + EARLIER
    row_places, col_places = lax.axis_size("row"), lax.axis_size("col")
    rounds, cols = len(swaps(row_places)), len(swaps(col_places))
    whole = row_places == 2 and cols == 2 and height == 2 * RIM
    payload = [] if whole else [((total, RIM, breadth, width), BF)] * rounds
    field, *sends = call(
        functools.partial(join_frames, pieces=pieces),
        [((total, height, breadth, width), BF)] + payload,
        [latent, ready, *got], flops=COVER,
    )
    rows_got = exchange([field] if whole else sends, "row")
    tall = height + 2 * RIM
    sides = [((RIM, total * tall, width), BF)] * (1 if whole else cols)
    *sends, own = call(
        functools.partial(strips, rows=rounds, whole=whole),
        sides + [((2 * RIM, total * tall, width), BF)], [field, *rows_got],
        [(blocked(total * tall * breadth, width), F32)],
    )
    early = total - 2

    def inner(begin, count, *after):
        return call(
            functools.partial(first_inner, rows=rounds, whole=whole, begin=begin),
            [((count, tall - 2, breadth, mid), F32)], [field, *rows_got, w_first, *after],
            [((3, count + 2, tall, breadth, width), BF)],
            flops=2 * 27 * count * (tall - 2) * breadth * width * mid,
        )

    if whole:
        pairs = []
        for section in range(sections):
            for core, pairing in enumerate(swaps(col_places)):
                at = (section * row_places + core) * col_places
                for i, j in pairing:
                    if abs(i - j) > 1 and sections % 2 == 0:
                        to = ((section ^ 1) * row_places + core) * col_places
                        pairs.append((at + i, to + i))
                    else:
                        pairs.append((at + i, at + j))
        came = lax.ppermute(sends[0], ("section", "row", "col"), pairs)
        cut = 5 * early // 8
        inners = inner(0, cut)
        cols_got = [came, *exchange([came], "row")]
        inners += inner(cut, early - cut, came)
    else:
        cols_got = exchange(sends, "col")
        inners = inner(0, early)
    later, corners = early - 2, tall - 3
    size = early * tall
    near, far = call(
        functools.partial(first_outer, cols=cols, parts=len(inners), whole=whole),
        [((2, early, tall - 2, breadth, mid), BF), ((2, size + 8, mid), F32)],
        [*inners, own, *cols_got, w_first],
        [((4 * RIM, total * tall, width), BF), (blocked(size * (breadth + SLACK), mid), F32)],
        flops=10**9,
    )
    (second,) = call(
        second_conv, [((2, 2 * corners, later, breadth, 2 * fine), BF)], [near, far, summed],
        [(blocked(later * tall * (breadth + SLACK), 4 * fine), F32)],
        flops=2 * 10**9,
    )
    steps = 2 if frames % 2 == 0 else 1
    (out,) = call(
        third_conv, [((frames, 2 * height, 2 * breadth, last), BF)], [second, paired],
        [
            ((frames // steps, 2 * height, 2 * breadth, last), F32),
            ((frames, 2 * height, 2 * breadth, last), BF), pltpu.SemaphoreType.DMA((steps,)),
        ],
        flops=10**9, to=pl.ANY,
    )
    return out


def solution(mesh):
    in_specs = (P("section", "row", "col", None), P(), P(), P())
    out_specs = P("section", "row", "col", None)

    return jax.shard_map(
        per_device, mesh=mesh, in_specs=in_specs, out_specs=out_specs, check_vma=False
    )
```

```python
import functools

import jax
import jax.numpy as jnp
from jax import lax
from jax.experimental import pallas as pl
from jax.experimental.pallas import tpu as pltpu
from jax.sharding import PartitionSpec as P


BF, F32 = jnp.bfloat16, jnp.float32
EARLIER = 6
RIM = 2


def call(body, outs, args, scratch=(), flops=0, to=pltpu.VMEM):
    spec = pl.BlockSpec(memory_space=pltpu.VMEM)
    outs = [jax.ShapeDtypeStruct(shape, kind) for shape, kind in outs]
    size = sum(a.size * a.dtype.itemsize for a in [*args, *outs])
    return pl.pallas_call(
        body, out_shape=outs, in_specs=[spec] * len(args),
        out_specs=[pl.BlockSpec(memory_space=to)] * len(outs),
        scratch_shapes=[pltpu.VMEM(*s) if isinstance(s, tuple) else s for s in scratch],
        cost_estimate=pl.CostEstimate(flops=flops, bytes_accessed=size, transcendentals=0),
        compiler_params=pltpu.CompilerParams(vmem_limit_bytes=32 << 20),
    )(*args)


LANES = 128
COVER = 4 * 10**9
SLACK = 8


def put(ref, rows, value):
    for k in range(ref.shape[0]):
        ref[k, rows, :] = value[:, k * LANES : (k + 1) * LANES]


def take(ref, rows, blocks=None):
    blocks = range(ref.shape[0]) if blocks is None else blocks
    return jnp.concatenate([ref[k, rows, :] for k in blocks], 1)


def blocked(rows, width):
    return (width // LANES, rows, LANES)


def swaps(size):
    assert size % 2 == 0
    rounds = [[(i, i + 1) for i in range(0, size, 2)]]
    if size > 2:
        rounds.append([(i, (i + 1) % size) for i in range(1, size, 2)])
    return [pairs + [(j, i) for i, j in pairs] for pairs in rounds]


def exchange(sends, axis):
    return [lax.ppermute(s, axis, pairs) for s, pairs in zip(sends, swaps(lax.axis_size(axis)))]


def column_exchange(sends, sections):
    rows, cols = lax.axis_size("row"), lax.axis_size("col")
    got = []
    for send, pairing in zip(sends, swaps(cols)):
        pairs = []
        for group in range(sections * rows):
            section, row = divmod(group, rows)
            for i, j in pairing:
                far = abs(i - j) > 1 and sections % 2 == 0
                to = ((section ^ 1) * rows + row, i) if far else (group, j)
                pairs.append((group * cols + i, to[0] * cols + to[1]))
        got.append(lax.ppermute(send, ("section", "row", "col"), pairs))
    return got


def arrived(axis, got):
    place, size = lax.axis_index(axis), lax.axis_size(axis)
    even = place % 2 == 0
    if len(got) == 1:
        before = after = got[0]
    else:
        before, after = jnp.where(even, got[1], got[0]), jnp.where(even, got[0], got[1])
    zero = jnp.zeros_like(before)
    return jnp.where(place > 0, before, zero), jnp.where(place < size - 1, after, zero)


def lead(out):
    out[...] = jnp.zeros_like(out)


def tails(latent, lead, *outs):
    for out in outs:
        out[...] = latent[latent.shape[0] - out.shape[0] :]


def send_rows(field, sends):
    even = lax.axis_index("row") % 2 == 0
    last = field.shape[1] - RIM
    for k, send in enumerate(sends):
        start = jnp.where(even, 0, last) if k else jnp.where(even, last, 0)
        send[...] = field[:, pl.ds(start, RIM)]


def own_rows(latent, lead, *sends):
    send_rows(latent, sends)


def join_frames(*refs, pieces):
    got = refs[1 : 1 + len(pieces)]
    field, sends = refs[1 + len(pieces)], refs[2 + len(pieces) :]
    place, at = lax.axis_index("section"), 0
    for (take, by), ref in zip(pieces, got):
        field[at : at + take] = jnp.where(place >= by, ref[...], jnp.zeros_like(ref))
        at += take
    send_rows(field, sends)


def strips(fields, out, wide, narrow):
    tall, breadth, width = fields[0].shape[1:]
    size, at = tall * breadth, 0
    for field in fields:
        for t in range(field.shape[0]):
            put(wide, slice(at, at + size), field[t].astype(F32).reshape(size, width))
            at += size
    frames = at // size
    for i, c in enumerate([0, 1, breadth - 2, breadth - 1]):
        for r in range(tall):
            narrow[r * frames : (r + 1) * frames] = take(
                wide, pl.ds(r * breadth + c, frames, stride=size)
            )
        out[i] = narrow[...].astype(BF)


def send_columns(before, latent, *refs):
    sends, own, wide, narrow = refs[:-3], refs[-3], refs[-2], refs[-1]
    strips([before, latent], own, wide, narrow)
    right = lax.axis_index("col") % 2 == 0
    for k, send in enumerate(sends):
        start = jnp.where(right, 0, RIM) if k else jnp.where(right, RIM, 0)
        send[...] = own[pl.ds(start, RIM)]


def rim_columns(*refs, rows):
    own, wide, narrow = refs[-3:]
    fields = []
    for got in (refs[:rows], refs[rows : 2 * rows]):
        fields.append(jnp.concatenate(arrived("row", [g[...] for g in got]), 1))
    strips(fields, own, wide, narrow)


def turn_columns(*refs, cols, frames):
    got, side, sends, narrow = refs[:cols], refs[cols + 1], refs[cols + 2 : -1], refs[-1]
    before, after = arrived("col", [g[...] for g in got])
    even = lax.axis_index("row") % 2 == 0
    size = RIM * frames
    for i, strip in enumerate([before[0], before[1], after[0], after[1]]):
        side[i] = strip
        narrow[...] = strip.astype(F32)
        first, last = narrow[:size], narrow[narrow.shape[0] - size :]
        for k, send in enumerate(sends):
            value = jnp.where(even, first, last) if k else jnp.where(even, last, first)
            send[i] = value.astype(BF)


def first_inner(*refs, sources, rows, begin):
    out, wide = refs[-2:]
    kernel = refs[sources * (1 + rows)]
    count = out.shape[0]
    frames = []
    for k in range(sources):
        field, *got = refs[k * (1 + rows) : (k + 1) * (1 + rows)]
        before, after = arrived("row", [g[...] for g in got])
        frames += [(before, field, after, t) for t in range(field.shape[0])]
    height, breadth, width = frames[0][1].shape[1:]
    tall = height + 2 * RIM
    size = tall * breadth
    col = lax.broadcasted_iota(jnp.int32, (size, width), 0) % breadth
    for t in range(count + 2):
        *parts, at = frames[begin + t]
        rows_of = jnp.concatenate([part[at] for part in parts], 0)
        wide[1, t] = rows_of
        flat = rows_of.reshape(size, width).astype(F32)
        lower = jnp.where(col == 0, 0.0, pltpu.roll(flat, 1, 0))
        upper = jnp.where(col == breadth - 1, 0.0, pltpu.roll(flat, size - 1, 0))
        wide[0, t] = lower.astype(BF).reshape(rows_of.shape)
        wide[2, t] = upper.astype(BF).reshape(rows_of.shape)
    taps = [
        wide[e, a : a + count, b : b + tall - 2].reshape(-1, width)
        for a in range(3) for b in range(3) for e in range(3)
    ]
    found = jnp.dot(
        jnp.concatenate(taps, 1), kernel[...].reshape(-1, kernel.shape[-1]), preferred_element_type=F32
    )
    out[...] = found.reshape(out.shape)


def kernels(second, third, summed, paired, ready):
    ready[...] = jnp.zeros_like(ready)
    fine = second.shape[-1]
    reads = [[(0, 1), (2,)], [(0,), (1, 2)]]
    for a in range(3):
        tap = [[second[a, b, e].astype(F32) for e in range(3)] for b in range(3)]
        for di in range(2):
            for dj in range(2):
                for py in range(2):
                    for px in range(2):
                        parts = [tap[b][e] for b in reads[py][di] for e in reads[px][dj]]
                        at = (2 * py + px) * fine
                        summed[a, di, dj, :, at : at + fine] = sum(parts[1:], parts[0]).astype(BF)
    width, out = third.shape[-2:]
    for a in range(3):
        for b in range(3):
            for dj in range(2):
                for px in range(2):
                    for q in range(2):
                        e = 2 * dj + px - q
                        block = third[a, b, e] if 0 <= e < 3 else jnp.zeros((width, out), BF)
                        paired[a, b, dj, px * width : (px + 1) * width, q * out : (q + 1) * out] = block


def limits(axis):
    return lax.axis_index(axis) == 0, lax.axis_index(axis) == lax.axis_size(axis) - 1


def first_outer(*refs, parts, rounds):
    inner, own, rim, side = refs[:parts], *refs[parts : parts + 3]
    turned = refs[parts + 3 : parts + 3 + rounds]
    kernel, near, far, edge, moved, coarse = refs[parts + 3 + rounds :]
    rows, breadth, width = inner[0].shape[1:]
    frames = sum(part.shape[0] for part in inner)
    total, tall = frames + 2, rows + 2
    (top, bottom), (leftmost, rightmost) = limits("row"), limits("col")

    above, below = arrived("row", [g[...] for g in turned])
    ends = RIM * total
    full = tall * total
    for i in range(RIM):
        for k, (main, at) in enumerate([(side, i), (own, i), (own, RIM + i), (side, RIM + i)]):
            strip = edge.at[k * RIM + i]
            strip[ends : full - ends] = main[at].astype(F32)
            if main is own:
                strip[:ends] = rim[at, :ends].astype(F32)
                strip[full - ends : full] = rim[at, ends : 2 * ends].astype(F32)
            else:
                strip[:ends] = above[at].astype(F32)
                strip[full - ends : full] = below[at].astype(F32)
    for i in range(4 * RIM):
        for a in range(3):
            moved[i, a] = jnp.concatenate(
                [edge[i, r * total + a : r * total + a + frames] for r in range(tall)], 0
            ).astype(BF)
    size = rows * frames
    lhs = jnp.concatenate([
        jnp.concatenate(
            [moved[i + e, a, b * frames : b * frames + size] for i in (0, 1, 4, 5)], 0
        )
        for a in range(3) for b in range(3) for e in range(3)
    ], 1)
    found = jnp.dot(lhs, kernel[...].reshape(-1, kernel.shape[-1]), preferred_element_type=F32)
    left, begin, end, right = [found[i * size : (i + 1) * size] for i in range(4)]

    pitch = breadth + SLACK
    count = 0
    for part in inner:
        for t in range(part.shape[0]):
            for r in range(rows):
                at = (r * frames + count) * pitch
                put(coarse, slice(at, at + breadth), part[t, r])
            count += 1
    put(coarse, pl.ds(0, size, stride=pitch), begin)
    put(coarse, pl.ds(breadth - 1, size, stride=pitch), end)
    put(coarse, pl.ds(breadth, size, stride=pitch), right)

    slot = lax.broadcasted_iota(jnp.int32, (breadth, width), 0)
    ends = rightmost & (slot == breadth - 1)
    for r in range(rows):
        lost = top if r == 0 else bottom if r == rows - 1 else None
        for t in range(frames):
            at = (r * frames + t) * pitch
            for dj in range(2):
                value = jnp.maximum(take(coarse, slice(at + dj, at + dj + breadth)), 0.0)
                gone = [g for g in (lost, ends if dj else None) if g is not None]
                if gone:
                    value = jnp.where(functools.reduce(jnp.logical_or, gone), 0.0, value)
                near[dj, r, t] = value.astype(BF)
    row = lax.broadcasted_iota(jnp.int32, (size, width), 0) // frames
    outside = (top & (row == 0)) | (bottom & (row == rows - 1))
    far[0, :size] = jnp.where(outside | leftmost, 0.0, jnp.maximum(left, 0.0))
    far[1, :size] = jnp.where(outside, 0.0, jnp.maximum(begin, 0.0))


def second_conv(near, far, summed, fine, grown):
    _, rows, frames, breadth, width = near.shape
    pitch = breadth + SLACK
    (top, bottom), (leftmost, rightmost) = limits("row"), limits("col")
    corners, later = rows - 1, frames - 2
    short = corners * frames
    taps = [
        jnp.concatenate([
            near[dj, di : di + corners, a : a + later].reshape(-1, width),
            far[dj, di * frames + a : di * frames + a + short].astype(BF),
        ], 0)
        for a in range(3) for di in range(2) for dj in range(2)
    ]
    found = jnp.dot(
        jnp.concatenate(taps, 1), summed[...].reshape(-1, summed.shape[-1]), preferred_element_type=F32
    )
    found = jnp.maximum(found, 0.0)
    full = later * corners * breadth
    half = found.shape[1] // 2
    for i in range(corners):
        for t in range(later):
            at, to = (i * later + t) * breadth, (i * frames + t) * pitch + SLACK
            put(grown, slice(to, to + breadth), found[at : at + breadth])
    put(grown, pl.ds(SLACK - 1, short, stride=pitch), found[full:])
    slot = lax.broadcasted_iota(jnp.int32, (breadth, half), 0)
    side = lax.broadcasted_iota(jnp.int32, (breadth, half), 1) < half // 2
    begins = leftmost & (slot == 0) & side
    ends = rightmost & (slot == breadth - 1) & ~side
    for t in range(later):
        for i in range(corners):
            for py in range(2):
                blocks = range(py * half // LANES, (py + 1) * half // LANES)
                lost = (top if py == 0 and i == 0 else bottom if py == 1 and i == corners - 1 else None)
                for dj, gone in enumerate((begins, ends)):
                    gone = gone if lost is None else gone | lost
                    at = (i * frames + t) * pitch + SLACK - 1 + dj
                    value = take(grown, slice(at, at + breadth), blocks)
                    fine[dj, 2 * i + py, t] = jnp.where(gone, 0.0, value).astype(BF)


def third_conv(fine, paired, out, spread, ready, sems):
    _, high, later, breadth, half = fine.shape
    high, kept, wide = high - 2, later - 2, out.shape[-1]
    steps = sems.shape[0]
    count = kept // steps

    def leave(step):
        mine = pl.ds(step * count, count)
        return pltpu.make_async_copy(ready.at[mine], out.at[mine], sems.at[step])

    @pl.loop(0, steps)
    def _(step):
        begin = step * count
        taps = [
            fine[dj, b : b + high, pl.ds(begin + a, count)].reshape(-1, half)
            for a in range(3) for b in range(3) for dj in range(2)
        ]
        kernel = paired[...].reshape(-1, paired.shape[-1])
        found = jnp.dot(jnp.concatenate(taps, 1), kernel, preferred_element_type=F32)
        for y in range(high):
            for t in range(count):
                at = (y * count + t) * breadth
                for q in range(2):
                    spread[t, y, pl.ds(q, breadth, stride=2), :] = found[
                        at : at + breadth, q * wide : (q + 1) * wide
                    ]
        ready[pl.ds(begin, count)] = spread[...].astype(BF)
        leave(step).start()

    for step in range(steps):
        leave(step).wait()


def per_device(latent, w_first, w_second, w_third):
    frames, height, breadth, width = latent.shape
    mid, fine = w_first.shape[-1], w_second.shape[-1]
    last = w_third.shape[-1]
    sections = lax.axis_size("section")
    pieces, left, by = [], EARLIER, 1
    while left > 0:
        pieces.insert(0, (min(left, frames), by))
        left, by = left - frames, by + 1
    (first_of_all,) = call(lead, [((8, LANES), F32)], [], flops=COVER)
    part = [take for take, _ in pieces if take < frames]
    ends = []
    if part:
        ends = list(call(
            tails, [((take, height, breadth, width), BF) for take in part],
            [latent, first_of_all],
        ))
    got = []
    for take, by in pieces:
        ring = [(i, (i + by) % sections) for i in range(sections)]
        got.append(lax.ppermute(ends.pop(0) if take < frames else latent, "section", ring))

    rounds, cols = len(swaps(lax.axis_size("row"))), len(swaps(lax.axis_size("col")))
    total, tall = frames + EARLIER, height + 2 * RIM
    early = total - 2
    sends = call(own_rows, [((frames, RIM, breadth, width), BF)] * rounds, [latent, first_of_all])
    own_got = exchange(sends, "row")
    summed, paired, ready = call(
        kernels,
        [((3, 2, 2, mid, 4 * fine), BF), ((3, 3, 2, 2 * fine, 2 * last), BF), ((8, LANES), F32)],
        [w_second, w_third], flops=COVER,
    )

    def inner(fields, begin, count, *after):
        return call(
            functools.partial(first_inner, sources=len(fields), rows=rounds, begin=begin),
            [((count, tall - 2, breadth, mid), F32)],
            [a for field, rim in fields for a in (field, *rim)] + [w_first, *after],
            [((3, count + 2, tall, breadth, width), BF)],
            flops=2 * 27 * count * (tall - 2) * breadth * width * mid,
        )

    inners = inner([(latent, own_got)], 0, frames - 2, ready)
    earlier, *sends = call(
        functools.partial(join_frames, pieces=pieces),
        [((EARLIER, height, breadth, width), BF)] + [((EARLIER, RIM, breadth, width), BF)] * rounds,
        [inners[0], *got],
    )
    early_got = exchange(sends, "row")
    strip = ((2 * RIM, height * total, width), BF)
    scratch = [(blocked(total * height * breadth, width), F32), ((height * total, width), F32)]
    *sends, own = call(
        send_columns, [((RIM, height * total, width), BF)] * cols + [strip], [earlier, latent],
        scratch,
    )
    came = column_exchange(sends, sections)
    fields = [(earlier, early_got), (latent, own_got)]
    rest = early - (frames - 2)
    cut = rest // 2
    first_part = inner(fields, 0, cut, *sends)
    side, *sends = call(
        functools.partial(turn_columns, cols=cols, frames=total),
        [strip] + [((2 * RIM, RIM * total, width), BF)] * rounds, [*came, *first_part],
        [((height * total, width), F32)],
    )
    turned = exchange(sends, "row")
    (rim,) = call(
        functools.partial(rim_columns, rows=rounds), [strip], [*early_got, *own_got, side],
        scratch,
    )
    inners = first_part + inner(fields, cut, rest - cut, side) + inners
    size = (tall - 2) * early
    near, far = call(
        functools.partial(first_outer, parts=len(inners), rounds=rounds),
        [((2, tall - 2, early, breadth, mid), BF), ((2, size + 8, mid), F32)],
        [*inners, own, rim, side, *turned, w_first],
        [
            ((4 * RIM, tall * total, width), F32), ((4 * RIM, 3, tall * early, width), BF),
            (blocked(size * (breadth + SLACK), mid), F32),
        ],
        flops=10**9,
    )
    later, corners = early - 2, tall - 3
    (second,) = call(
        second_conv, [((2, 2 * corners, later, breadth, 2 * fine), BF)], [near, far, summed],
        [(blocked(corners * early * (breadth + SLACK), 4 * fine), F32)],
        flops=2 * 10**9,
    )
    steps = 2 if frames % 2 == 0 else 1
    (out,) = call(
        third_conv, [((frames, 2 * height, 2 * breadth, last), BF)], [second, paired],
        [
            ((frames // steps, 2 * height, 2 * breadth, last), F32),
            ((frames, 2 * height, 2 * breadth, last), BF), pltpu.SemaphoreType.DMA((steps,)),
        ],
        flops=10**9, to=pl.ANY,
    )
    return out


def solution(mesh):
    in_specs = (P("section", "row", "col", None), P(), P(), P())
    out_specs = P("section", "row", "col", None)

    return jax.shard_map(
        per_device, mesh=mesh, in_specs=in_specs, out_specs=out_specs, check_vma=False
    )
```

```python
import functools

import jax
import jax.numpy as jnp
from jax import lax
from jax.experimental import pallas as pl
from jax.experimental.pallas import tpu as pltpu
from jax.sharding import PartitionSpec as P


BF, F32 = jnp.bfloat16, jnp.float32
EARLIER = 6
RIM = 2


def call(body, outs, args, scratch=(), flops=0):
    spec = pl.BlockSpec(memory_space=pltpu.VMEM)
    outs = [jax.ShapeDtypeStruct(shape, kind) for shape, kind in outs]
    size = sum(a.size * a.dtype.itemsize for a in [*args, *outs])
    return pl.pallas_call(
        body, out_shape=outs, in_specs=[spec] * len(args), out_specs=[spec] * len(outs),
        scratch_shapes=[pltpu.VMEM(*s) for s in scratch],
        cost_estimate=pl.CostEstimate(flops=flops, bytes_accessed=size, transcendentals=0),
        compiler_params=pltpu.CompilerParams(vmem_limit_bytes=32 << 20),
    )(*args)


LANES = 128
COVER = 4 * 10**9
SLACK = 8


def put(ref, rows, value):
    for k in range(ref.shape[0]):
        ref[k, rows, :] = value[:, k * LANES : (k + 1) * LANES]


def take(ref, rows, blocks=None):
    blocks = range(ref.shape[0]) if blocks is None else blocks
    return jnp.concatenate([ref[k, rows, :] for k in blocks], 1)


def blocked(rows, width):
    return (width // LANES, rows, LANES)


def swaps(size):
    assert size % 2 == 0
    rounds = [[(i, i + 1) for i in range(0, size, 2)]]
    if size > 2:
        rounds.append([(i, (i + 1) % size) for i in range(1, size, 2)])
    return [pairs + [(j, i) for i, j in pairs] for pairs in rounds]


def exchange(sends, axis):
    return [lax.ppermute(s, axis, pairs) for s, pairs in zip(sends, swaps(lax.axis_size(axis)))]


def column_exchange(sends, sections):
    rows, cols = lax.axis_size("row"), lax.axis_size("col")
    got = []
    for send, pairing in zip(sends, swaps(cols)):
        pairs = []
        for group in range(sections * rows):
            section, row = divmod(group, rows)
            for i, j in pairing:
                far = abs(i - j) > 1 and sections % 2 == 0
                to = ((section ^ 1) * rows + row, i) if far else (group, j)
                pairs.append((group * cols + i, to[0] * cols + to[1]))
        got.append(lax.ppermute(send, ("section", "row", "col"), pairs))
    return got


def arrived(axis, got):
    place, size = lax.axis_index(axis), lax.axis_size(axis)
    even = place % 2 == 0
    if len(got) == 1:
        before = after = got[0]
    else:
        before, after = jnp.where(even, got[1], got[0]), jnp.where(even, got[0], got[1])
    zero = jnp.zeros_like(before)
    return jnp.where(place > 0, before, zero), jnp.where(place < size - 1, after, zero)


def lead(out):
    out[...] = jnp.zeros_like(out)


def tails(latent, lead, *outs):
    for out in outs:
        out[...] = latent[latent.shape[0] - out.shape[0] :]


def send_rows(field, sends):
    even = lax.axis_index("row") % 2 == 0
    last = field.shape[1] - RIM
    for k, send in enumerate(sends):
        start = jnp.where(even, 0, last) if k else jnp.where(even, last, 0)
        send[...] = field[:, pl.ds(start, RIM)]


def own_rows(latent, lead, *sends):
    send_rows(latent, sends)


def join_frames(*refs, pieces):
    got = refs[1 : 1 + len(pieces)]
    field, sends = refs[1 + len(pieces)], refs[2 + len(pieces) :]
    place, at = lax.axis_index("section"), 0
    for (take, by), ref in zip(pieces, got):
        field[at : at + take] = jnp.where(place >= by, ref[...], jnp.zeros_like(ref))
        at += take
    send_rows(field, sends)


def strips(fields, out, wide, narrow):
    tall, breadth, width = fields[0].shape[1:]
    size, at = tall * breadth, 0
    for field in fields:
        for t in range(field.shape[0]):
            put(wide, slice(at, at + size), field[t].astype(F32).reshape(size, width))
            at += size
    frames = at // size
    for i, c in enumerate([0, 1, breadth - 2, breadth - 1]):
        for r in range(tall):
            narrow[r * frames : (r + 1) * frames] = take(
                wide, pl.ds(r * breadth + c, frames, stride=size)
            )
        out[i] = narrow[...].astype(BF)


def send_columns(before, latent, *refs):
    sends, own, wide, narrow = refs[:-3], refs[-3], refs[-2], refs[-1]
    strips([before, latent], own, wide, narrow)
    right = lax.axis_index("col") % 2 == 0
    for k, send in enumerate(sends):
        start = jnp.where(right, 0, RIM) if k else jnp.where(right, RIM, 0)
        send[...] = own[pl.ds(start, RIM)]


def rim_columns(*refs, rows):
    own, wide, narrow = refs[-3:]
    fields = []
    for got in (refs[:rows], refs[rows : 2 * rows]):
        fields.append(jnp.concatenate(arrived("row", [g[...] for g in got]), 1))
    strips(fields, own, wide, narrow)


def turn_columns(*refs, cols, frames):
    got, side, sends, narrow = refs[:cols], refs[cols + 1], refs[cols + 2 : -1], refs[-1]
    before, after = arrived("col", [g[...] for g in got])
    even = lax.axis_index("row") % 2 == 0
    size = RIM * frames
    for i, strip in enumerate([before[0], before[1], after[0], after[1]]):
        side[i] = strip
        narrow[...] = strip.astype(F32)
        first, last = narrow[:size], narrow[narrow.shape[0] - size :]
        for k, send in enumerate(sends):
            value = jnp.where(even, first, last) if k else jnp.where(even, last, first)
            send[i] = value.astype(BF)


def first_inner(*refs, sources, rows, begin):
    out, wide = refs[-2:]
    kernel = refs[sources * (1 + rows)]
    count = out.shape[0]
    frames = []
    for k in range(sources):
        field, *got = refs[k * (1 + rows) : (k + 1) * (1 + rows)]
        before, after = arrived("row", [g[...] for g in got])
        frames += [(before, field, after, t) for t in range(field.shape[0])]
    height, breadth, width = frames[0][1].shape[1:]
    tall = height + 2 * RIM
    size = tall * breadth
    col = lax.broadcasted_iota(jnp.int32, (size, width), 0) % breadth
    for t in range(count + 2):
        *parts, at = frames[begin + t]
        rows_of = jnp.concatenate([part[at] for part in parts], 0)
        wide[1, t] = rows_of
        flat = rows_of.reshape(size, width).astype(F32)
        lower = jnp.where(col == 0, 0.0, pltpu.roll(flat, 1, 0))
        upper = jnp.where(col == breadth - 1, 0.0, pltpu.roll(flat, size - 1, 0))
        wide[0, t] = lower.astype(BF).reshape(rows_of.shape)
        wide[2, t] = upper.astype(BF).reshape(rows_of.shape)
    taps = [
        wide[e, a : a + count, b : b + tall - 2].reshape(-1, width)
        for a in range(3) for b in range(3) for e in range(3)
    ]
    found = jnp.dot(
        jnp.concatenate(taps, 1), kernel[...].reshape(-1, kernel.shape[-1]), preferred_element_type=F32
    )
    out[...] = found.reshape(out.shape)


def kernels(second, third, summed, paired, ready):
    ready[...] = jnp.zeros_like(ready)
    fine = second.shape[-1]
    reads = [[(0, 1), (2,)], [(0,), (1, 2)]]
    for a in range(3):
        tap = [[second[a, b, e].astype(F32) for e in range(3)] for b in range(3)]
        for di in range(2):
            for dj in range(2):
                for py in range(2):
                    for px in range(2):
                        parts = [tap[b][e] for b in reads[py][di] for e in reads[px][dj]]
                        at = (2 * py + px) * fine
                        summed[a, di, dj, :, at : at + fine] = sum(parts[1:], parts[0]).astype(BF)
    width, out = third.shape[-2:]
    for a in range(3):
        for b in range(3):
            for dj in range(2):
                for px in range(2):
                    for q in range(2):
                        e = 2 * dj + px - q
                        block = third[a, b, e] if 0 <= e < 3 else jnp.zeros((width, out), BF)
                        paired[a, b, dj, px * width : (px + 1) * width, q * out : (q + 1) * out] = block


def limits(axis):
    return lax.axis_index(axis) == 0, lax.axis_index(axis) == lax.axis_size(axis) - 1


def first_outer(*refs, parts, rounds):
    inner, own, rim, side = refs[:parts], *refs[parts : parts + 3]
    turned = refs[parts + 3 : parts + 3 + rounds]
    kernel, near, far, edge, moved, coarse = refs[parts + 3 + rounds :]
    rows, breadth, width = inner[0].shape[1:]
    frames = sum(part.shape[0] for part in inner)
    total, tall = frames + 2, rows + 2
    (top, bottom), (leftmost, rightmost) = limits("row"), limits("col")

    above, below = arrived("row", [g[...] for g in turned])
    ends = RIM * total
    full = tall * total
    for i in range(RIM):
        for k, (main, at) in enumerate([(side, i), (own, i), (own, RIM + i), (side, RIM + i)]):
            strip = edge.at[k * RIM + i]
            strip[ends : full - ends] = main[at].astype(F32)
            if main is own:
                strip[:ends] = rim[at, :ends].astype(F32)
                strip[full - ends : full] = rim[at, ends : 2 * ends].astype(F32)
            else:
                strip[:ends] = above[at].astype(F32)
                strip[full - ends : full] = below[at].astype(F32)
    for i in range(4 * RIM):
        for a in range(3):
            moved[i, a] = jnp.concatenate(
                [edge[i, r * total + a : r * total + a + frames] for r in range(tall)], 0
            ).astype(BF)
    size = rows * frames
    lhs = jnp.concatenate([
        jnp.concatenate(
            [moved[i + e, a, b * frames : b * frames + size] for i in (0, 1, 4, 5)], 0
        )
        for a in range(3) for b in range(3) for e in range(3)
    ], 1)
    found = jnp.dot(lhs, kernel[...].reshape(-1, kernel.shape[-1]), preferred_element_type=F32)
    left, begin, end, right = [found[i * size : (i + 1) * size] for i in range(4)]

    pitch = breadth + SLACK
    count = 0
    for part in inner:
        for t in range(part.shape[0]):
            for r in range(rows):
                at = (r * frames + count) * pitch
                put(coarse, slice(at, at + breadth), part[t, r])
            count += 1
    put(coarse, pl.ds(0, size, stride=pitch), begin)
    put(coarse, pl.ds(breadth - 1, size, stride=pitch), end)
    put(coarse, pl.ds(breadth, size, stride=pitch), right)

    slot = lax.broadcasted_iota(jnp.int32, (breadth, width), 0)
    ends = rightmost & (slot == breadth - 1)
    for r in range(rows):
        lost = top if r == 0 else bottom if r == rows - 1 else None
        for t in range(frames):
            at = (r * frames + t) * pitch
            for dj in range(2):
                value = jnp.maximum(take(coarse, slice(at + dj, at + dj + breadth)), 0.0)
                gone = [g for g in (lost, ends if dj else None) if g is not None]
                if gone:
                    value = jnp.where(functools.reduce(jnp.logical_or, gone), 0.0, value)
                near[dj, r, t] = value.astype(BF)
    row = lax.broadcasted_iota(jnp.int32, (size, width), 0) // frames
    outside = (top & (row == 0)) | (bottom & (row == rows - 1))
    far[0, :size] = jnp.where(outside | leftmost, 0.0, jnp.maximum(left, 0.0))
    far[1, :size] = jnp.where(outside, 0.0, jnp.maximum(begin, 0.0))


def second_conv(near, far, summed, fine, grown):
    _, rows, frames, breadth, width = near.shape
    pitch = breadth + SLACK
    (top, bottom), (leftmost, rightmost) = limits("row"), limits("col")
    corners, later = rows - 1, frames - 2
    short = corners * frames
    taps = [
        jnp.concatenate([
            near[dj, di : di + corners, a : a + later].reshape(-1, width),
            far[dj, di * frames + a : di * frames + a + short].astype(BF),
        ], 0)
        for a in range(3) for di in range(2) for dj in range(2)
    ]
    found = jnp.dot(
        jnp.concatenate(taps, 1), summed[...].reshape(-1, summed.shape[-1]), preferred_element_type=F32
    )
    found = jnp.maximum(found, 0.0)
    full = later * corners * breadth
    half = found.shape[1] // 2
    for i in range(corners):
        for t in range(later):
            at, to = (i * later + t) * breadth, (i * frames + t) * pitch + SLACK
            put(grown, slice(to, to + breadth), found[at : at + breadth])
    put(grown, pl.ds(SLACK - 1, short, stride=pitch), found[full:])
    slot = lax.broadcasted_iota(jnp.int32, (breadth, half), 0)
    side = lax.broadcasted_iota(jnp.int32, (breadth, half), 1) < half // 2
    begins = leftmost & (slot == 0) & side
    ends = rightmost & (slot == breadth - 1) & ~side
    for t in range(later):
        for i in range(corners):
            for py in range(2):
                blocks = range(py * half // LANES, (py + 1) * half // LANES)
                lost = (top if py == 0 and i == 0 else bottom if py == 1 and i == corners - 1 else None)
                for dj, gone in enumerate((begins, ends)):
                    gone = gone if lost is None else gone | lost
                    at = (i * frames + t) * pitch + SLACK - 1 + dj
                    value = take(grown, slice(at, at + breadth), blocks)
                    fine[dj, 2 * i + py, t] = jnp.where(gone, 0.0, value).astype(BF)


def third_conv(fine, paired, out, spread):
    _, high, later, breadth, half = fine.shape
    high, kept, wide = high - 2, later - 2, out.shape[-1]
    kernel = paired[...].reshape(-1, paired.shape[-1])
    step = high // 2
    for begin in range(0, high, step):
        taps = [
            fine[dj, begin + b : begin + b + step, a : a + kept].reshape(-1, half)
            for a in range(3) for b in range(3) for dj in range(2)
        ]
        found = jnp.dot(jnp.concatenate(taps, 1), kernel, preferred_element_type=F32)
        for y in range(step):
            for t in range(kept):
                at = (y * kept + t) * breadth
                for q in range(2):
                    spread[t, begin + y, pl.ds(q, breadth, stride=2), :] = found[
                        at : at + breadth, q * wide : (q + 1) * wide
                    ]
    out[...] = spread[...].astype(BF)


def per_device(latent, w_first, w_second, w_third):
    frames, height, breadth, width = latent.shape
    mid, fine = w_first.shape[-1], w_second.shape[-1]
    last = w_third.shape[-1]
    sections = lax.axis_size("section")
    pieces, left, by = [], EARLIER, 1
    while left > 0:
        pieces.insert(0, (min(left, frames), by))
        left, by = left - frames, by + 1
    (first_of_all,) = call(lead, [((8, LANES), F32)], [], flops=COVER)
    part = [take for take, _ in pieces if take < frames]
    ends = []
    if part:
        ends = list(call(
            tails, [((take, height, breadth, width), BF) for take in part],
            [latent, first_of_all],
        ))
    got = []
    for take, by in pieces:
        ring = [(i, (i + by) % sections) for i in range(sections)]
        got.append(lax.ppermute(ends.pop(0) if take < frames else latent, "section", ring))

    rounds, cols = len(swaps(lax.axis_size("row"))), len(swaps(lax.axis_size("col")))
    total, tall = frames + EARLIER, height + 2 * RIM
    early = total - 2
    sends = call(own_rows, [((frames, RIM, breadth, width), BF)] * rounds, [latent, first_of_all])
    own_got = exchange(sends, "row")
    summed, paired, ready = call(
        kernels,
        [((3, 2, 2, mid, 4 * fine), BF), ((3, 3, 2, 2 * fine, 2 * last), BF), ((8, LANES), F32)],
        [w_second, w_third], flops=COVER,
    )

    def inner(fields, begin, count, *after):
        return call(
            functools.partial(first_inner, sources=len(fields), rows=rounds, begin=begin),
            [((count, tall - 2, breadth, mid), F32)],
            [a for field, rim in fields for a in (field, *rim)] + [w_first, *after],
            [((3, count + 2, tall, breadth, width), BF)],
            flops=2 * 27 * count * (tall - 2) * breadth * width * mid,
        )

    inners = inner([(latent, own_got)], 0, frames - 2, ready)
    earlier, *sends = call(
        functools.partial(join_frames, pieces=pieces),
        [((EARLIER, height, breadth, width), BF)] + [((EARLIER, RIM, breadth, width), BF)] * rounds,
        [inners[0], *got],
    )
    early_got = exchange(sends, "row")
    strip = ((2 * RIM, height * total, width), BF)
    scratch = [(blocked(total * height * breadth, width), F32), ((height * total, width), F32)]
    *sends, own = call(
        send_columns, [((RIM, height * total, width), BF)] * cols + [strip], [earlier, latent],
        scratch,
    )
    came = column_exchange(sends, sections)
    fields = [(earlier, early_got), (latent, own_got)]
    rest = early - (frames - 2)
    cut = rest // 2
    first_part = inner(fields, 0, cut, *sends)
    (rim,) = call(
        functools.partial(rim_columns, rows=rounds), [strip], [*early_got, *own_got, *first_part],
        scratch,
    )
    side, *sends = call(
        functools.partial(turn_columns, cols=cols, frames=total),
        [strip] + [((2 * RIM, RIM * total, width), BF)] * rounds, [*came, rim],
        [((height * total, width), F32)],
    )
    turned = exchange(sends, "row")
    inners = first_part + inner(fields, cut, rest - cut, side) + inners
    size = (tall - 2) * early
    near, far = call(
        functools.partial(first_outer, parts=len(inners), rounds=rounds),
        [((2, tall - 2, early, breadth, mid), BF), ((2, size + 8, mid), F32)],
        [*inners, own, rim, side, *turned, w_first],
        [
            ((4 * RIM, tall * total, width), F32), ((4 * RIM, 3, tall * early, width), BF),
            (blocked(size * (breadth + SLACK), mid), F32),
        ],
        flops=10**9,
    )
    later, corners = early - 2, tall - 3
    (second,) = call(
        second_conv, [((2, 2 * corners, later, breadth, 2 * fine), BF)], [near, far, summed],
        [(blocked(corners * early * (breadth + SLACK), 4 * fine), F32)],
        flops=2 * 10**9,
    )
    (out,) = call(
        third_conv, [((frames, 2 * height, 2 * breadth, last), BF)], [second, paired],
        [((frames, 2 * height, 2 * breadth, last), F32)], flops=10**9,
    )
    return out


def solution(mesh):
    in_specs = (P("section", "row", "col", None), P(), P(), P())
    out_specs = P("section", "row", "col", None)

    return jax.shard_map(
        per_device, mesh=mesh, in_specs=in_specs, out_specs=out_specs, check_vma=False
    )
```

```python
import functools

import jax
import jax.numpy as jnp
from jax import lax
from jax.experimental import pallas as pl
from jax.experimental.pallas import tpu as pltpu
from jax.sharding import PartitionSpec as P


BF, F32 = jnp.bfloat16, jnp.float32
EARLIER = 6
RIM = 2


def call(body, outs, args, scratch=(), flops=0):
    spec = pl.BlockSpec(memory_space=pltpu.VMEM)
    outs = [jax.ShapeDtypeStruct(shape, kind) for shape, kind in outs]
    size = sum(a.size * a.dtype.itemsize for a in [*args, *outs])
    return pl.pallas_call(
        body, out_shape=outs, in_specs=[spec] * len(args), out_specs=[spec] * len(outs),
        scratch_shapes=[pltpu.VMEM(*s) for s in scratch],
        cost_estimate=pl.CostEstimate(flops=flops, bytes_accessed=size, transcendentals=0),
        compiler_params=pltpu.CompilerParams(vmem_limit_bytes=32 << 20),
    )(*args)


LANES = 128
COVER = 4 * 10**9
SLACK = 8


def put(ref, rows, value):
    for k in range(ref.shape[0]):
        ref[k, rows, :] = value[:, k * LANES : (k + 1) * LANES]


def take(ref, rows, blocks=None):
    blocks = range(ref.shape[0]) if blocks is None else blocks
    return jnp.concatenate([ref[k, rows, :] for k in blocks], 1)


def blocked(rows, width):
    return (width // LANES, rows, LANES)


def swaps(size):
    assert size % 2 == 0
    rounds = [[(i, i + 1) for i in range(0, size, 2)]]
    if size > 2:
        rounds.append([(i, (i + 1) % size) for i in range(1, size, 2)])
    return [pairs + [(j, i) for i, j in pairs] for pairs in rounds]


def exchange(sends, axis):
    return [lax.ppermute(s, axis, pairs) for s, pairs in zip(sends, swaps(lax.axis_size(axis)))]


def column_exchange(sends, sections):
    rows, cols = lax.axis_size("row"), lax.axis_size("col")
    got = []
    for send, pairing in zip(sends, swaps(cols)):
        pairs = []
        for group in range(sections * rows):
            for i, j in pairing:
                to = (group ^ 1, i) if abs(i - j) > 1 else (group, j)
                pairs.append((group * cols + i, to[0] * cols + to[1]))
        got.append(lax.ppermute(send, ("section", "row", "col"), pairs))
    return got


def arrived(axis, got):
    place, size = lax.axis_index(axis), lax.axis_size(axis)
    even = place % 2 == 0
    if len(got) == 1:
        before = after = got[0]
    else:
        before, after = jnp.where(even, got[1], got[0]), jnp.where(even, got[0], got[1])
    zero = jnp.zeros_like(before)
    return jnp.where(place > 0, before, zero), jnp.where(place < size - 1, after, zero)


def lead(out):
    out[...] = jnp.zeros_like(out)


def tails(latent, lead, *outs):
    for out in outs:
        out[...] = latent[latent.shape[0] - out.shape[0] :]


def send_rows(field, sends):
    even = lax.axis_index("row") % 2 == 0
    last = field.shape[1] - RIM
    for k, send in enumerate(sends):
        start = jnp.where(even, 0, last) if k else jnp.where(even, last, 0)
        send[...] = field[:, pl.ds(start, RIM)]


def own_rows(latent, lead, *sends):
    send_rows(latent, sends)


def join_frames(*refs, pieces):
    got = refs[1 : 1 + len(pieces)]
    field, sends = refs[1 + len(pieces)], refs[2 + len(pieces) :]
    place, at = lax.axis_index("section"), 0
    for (take, by), ref in zip(pieces, got):
        field[at : at + take] = jnp.where(place >= by, ref[...], jnp.zeros_like(ref))
        at += take
    send_rows(field, sends)


def strips(fields, out, wide, narrow):
    tall, breadth, width = fields[0].shape[1:]
    size, at = tall * breadth, 0
    for field in fields:
        for t in range(field.shape[0]):
            put(wide, slice(at, at + size), field[t].astype(F32).reshape(size, width))
            at += size
    frames = at // size
    for i, c in enumerate([0, 1, breadth - 2, breadth - 1]):
        for r in range(tall):
            narrow[r * frames : (r + 1) * frames] = take(
                wide, pl.ds(r * breadth + c, frames, stride=size)
            )
        out[i] = narrow[...].astype(BF)


def send_columns(before, latent, *refs):
    sends, own, wide, narrow = refs[:-3], refs[-3], refs[-2], refs[-1]
    strips([before, latent], own, wide, narrow)
    right = lax.axis_index("col") % 2 == 0
    for k, send in enumerate(sends):
        start = jnp.where(right, 0, RIM) if k else jnp.where(right, RIM, 0)
        send[...] = own[pl.ds(start, RIM)]


def rim_columns(*refs, rows):
    own, wide, narrow = refs[-3:]
    fields = []
    for got in (refs[:rows], refs[rows : 2 * rows]):
        fields.append(jnp.concatenate(arrived("row", [g[...] for g in got]), 1))
    strips(fields, own, wide, narrow)


def turn_columns(*refs, cols, frames):
    got, side, sends, narrow = refs[:cols], refs[cols + 1], refs[cols + 2 : -1], refs[-1]
    before, after = arrived("col", [g[...] for g in got])
    even = lax.axis_index("row") % 2 == 0
    size = RIM * frames
    for i, strip in enumerate([before[0], before[1], after[0], after[1]]):
        side[i] = strip
        narrow[...] = strip.astype(F32)
        first, last = narrow[:size], narrow[narrow.shape[0] - size :]
        for k, send in enumerate(sends):
            value = jnp.where(even, first, last) if k else jnp.where(even, last, first)
            send[i] = value.astype(BF)


def first_inner(*refs, sources, rows, begin):
    out, wide = refs[-2:]
    kernel = refs[sources * (1 + rows)]
    count = out.shape[0]
    frames = []
    for k in range(sources):
        field, *got = refs[k * (1 + rows) : (k + 1) * (1 + rows)]
        before, after = arrived("row", [g[...] for g in got])
        frames += [(before, field, after, t) for t in range(field.shape[0])]
    height, breadth, width = frames[0][1].shape[1:]
    tall = height + 2 * RIM
    size = tall * breadth
    col = lax.broadcasted_iota(jnp.int32, (size, width), 0) % breadth
    for t in range(count + 2):
        *parts, at = frames[begin + t]
        rows_of = jnp.concatenate([part[at] for part in parts], 0)
        wide[1, t] = rows_of
        flat = rows_of.reshape(size, width).astype(F32)
        lower = jnp.where(col == 0, 0.0, pltpu.roll(flat, 1, 0))
        upper = jnp.where(col == breadth - 1, 0.0, pltpu.roll(flat, size - 1, 0))
        wide[0, t] = lower.astype(BF).reshape(rows_of.shape)
        wide[2, t] = upper.astype(BF).reshape(rows_of.shape)
    taps = [
        wide[e, a : a + count, b : b + tall - 2].reshape(-1, width)
        for a in range(3) for b in range(3) for e in range(3)
    ]
    found = jnp.dot(
        jnp.concatenate(taps, 1), kernel[...].reshape(-1, kernel.shape[-1]), preferred_element_type=F32
    )
    out[...] = found.reshape(out.shape)


def kernels(second, third, summed, paired, ready):
    ready[...] = jnp.zeros_like(ready)
    fine = second.shape[-1]
    reads = [[(0, 1), (2,)], [(0,), (1, 2)]]
    for a in range(3):
        tap = [[second[a, b, e].astype(F32) for e in range(3)] for b in range(3)]
        for di in range(2):
            for dj in range(2):
                for py in range(2):
                    for px in range(2):
                        parts = [tap[b][e] for b in reads[py][di] for e in reads[px][dj]]
                        at = (2 * py + px) * fine
                        summed[a, di, dj, :, at : at + fine] = sum(parts[1:], parts[0]).astype(BF)
    width, out = third.shape[-2:]
    for a in range(3):
        for b in range(3):
            for dj in range(2):
                for px in range(2):
                    for q in range(2):
                        e = 2 * dj + px - q
                        block = third[a, b, e] if 0 <= e < 3 else jnp.zeros((width, out), BF)
                        paired[a, b, dj, px * width : (px + 1) * width, q * out : (q + 1) * out] = block


def limits(axis):
    return lax.axis_index(axis) == 0, lax.axis_index(axis) == lax.axis_size(axis) - 1


def first_outer(*refs, parts, rounds):
    inner, own, rim, side = refs[:parts], *refs[parts : parts + 3]
    turned = refs[parts + 3 : parts + 3 + rounds]
    kernel, near, far, edge, moved, coarse = refs[parts + 3 + rounds :]
    rows, breadth, width = inner[0].shape[1:]
    frames = sum(part.shape[0] for part in inner)
    total, tall = frames + 2, rows + 2
    (top, bottom), (leftmost, rightmost) = limits("row"), limits("col")

    above, below = arrived("row", [g[...] for g in turned])
    ends = RIM * total
    full = tall * total
    for i in range(RIM):
        for k, (main, at) in enumerate([(side, i), (own, i), (own, RIM + i), (side, RIM + i)]):
            strip = edge.at[k * RIM + i]
            strip[ends : full - ends] = main[at].astype(F32)
            if main is own:
                strip[:ends] = rim[at, :ends].astype(F32)
                strip[full - ends : full] = rim[at, ends : 2 * ends].astype(F32)
            else:
                strip[:ends] = above[at].astype(F32)
                strip[full - ends : full] = below[at].astype(F32)
    for i in range(4 * RIM):
        for a in range(3):
            moved[i, a] = jnp.concatenate(
                [edge[i, r * total + a : r * total + a + frames] for r in range(tall)], 0
            ).astype(BF)
    size = rows * frames
    lhs = jnp.concatenate([
        jnp.concatenate(
            [moved[i + e, a, b * frames : b * frames + size] for i in (0, 1, 4, 5)], 0
        )
        for a in range(3) for b in range(3) for e in range(3)
    ], 1)
    found = jnp.dot(lhs, kernel[...].reshape(-1, kernel.shape[-1]), preferred_element_type=F32)
    left, begin, end, right = [found[i * size : (i + 1) * size] for i in range(4)]

    pitch = breadth + SLACK
    count = 0
    for part in inner:
        for t in range(part.shape[0]):
            for r in range(rows):
                at = (r * frames + count) * pitch
                put(coarse, slice(at, at + breadth), part[t, r])
            count += 1
    put(coarse, pl.ds(0, size, stride=pitch), begin)
    put(coarse, pl.ds(breadth - 1, size, stride=pitch), end)
    put(coarse, pl.ds(breadth, size, stride=pitch), right)

    slot = lax.broadcasted_iota(jnp.int32, (breadth, width), 0)
    ends = rightmost & (slot == breadth - 1)
    for r in range(rows):
        lost = top if r == 0 else bottom if r == rows - 1 else None
        for t in range(frames):
            at = (r * frames + t) * pitch
            for dj in range(2):
                value = jnp.maximum(take(coarse, slice(at + dj, at + dj + breadth)), 0.0)
                gone = [g for g in (lost, ends if dj else None) if g is not None]
                if gone:
                    value = jnp.where(functools.reduce(jnp.logical_or, gone), 0.0, value)
                near[dj, r, t] = value.astype(BF)
    row = lax.broadcasted_iota(jnp.int32, (size, width), 0) // frames
    outside = (top & (row == 0)) | (bottom & (row == rows - 1))
    far[0, :size] = jnp.where(outside | leftmost, 0.0, jnp.maximum(left, 0.0))
    far[1, :size] = jnp.where(outside, 0.0, jnp.maximum(begin, 0.0))


def second_conv(near, far, summed, fine, grown):
    _, rows, frames, breadth, width = near.shape
    pitch = breadth + SLACK
    (top, bottom), (leftmost, rightmost) = limits("row"), limits("col")
    corners, later = rows - 1, frames - 2
    short = corners * frames
    taps = [
        jnp.concatenate([
            near[dj, di : di + corners, a : a + later].reshape(-1, width),
            far[dj, di * frames + a : di * frames + a + short].astype(BF),
        ], 0)
        for a in range(3) for di in range(2) for dj in range(2)
    ]
    found = jnp.dot(
        jnp.concatenate(taps, 1), summed[...].reshape(-1, summed.shape[-1]), preferred_element_type=F32
    )
    found = jnp.maximum(found, 0.0)
    full = later * corners * breadth
    half = found.shape[1] // 2
    for i in range(corners):
        for t in range(later):
            at, to = (i * later + t) * breadth, (i * frames + t) * pitch + SLACK
            put(grown, slice(to, to + breadth), found[at : at + breadth])
    put(grown, pl.ds(SLACK - 1, short, stride=pitch), found[full:])
    slot = lax.broadcasted_iota(jnp.int32, (breadth, half), 0)
    side = lax.broadcasted_iota(jnp.int32, (breadth, half), 1) < half // 2
    begins = leftmost & (slot == 0) & side
    ends = rightmost & (slot == breadth - 1) & ~side
    for t in range(later):
        for i in range(corners):
            for py in range(2):
                blocks = range(py * half // LANES, (py + 1) * half // LANES)
                lost = (top if py == 0 and i == 0 else bottom if py == 1 and i == corners - 1 else None)
                for dj, gone in enumerate((begins, ends)):
                    gone = gone if lost is None else gone | lost
                    at = (i * frames + t) * pitch + SLACK - 1 + dj
                    value = take(grown, slice(at, at + breadth), blocks)
                    fine[dj, 2 * i + py, t] = jnp.where(gone, 0.0, value).astype(BF)


def third_conv(fine, paired, out, spread):
    _, high, later, breadth, half = fine.shape
    high, kept, wide = high - 2, later - 2, out.shape[-1]
    kernel = paired[...].reshape(-1, paired.shape[-1])
    step = high // 2
    for begin in range(0, high, step):
        taps = [
            fine[dj, begin + b : begin + b + step, a : a + kept].reshape(-1, half)
            for a in range(3) for b in range(3) for dj in range(2)
        ]
        found = jnp.dot(jnp.concatenate(taps, 1), kernel, preferred_element_type=F32)
        for y in range(step):
            for t in range(kept):
                at = (y * kept + t) * breadth
                for q in range(2):
                    spread[t, begin + y, pl.ds(q, breadth, stride=2), :] = found[
                        at : at + breadth, q * wide : (q + 1) * wide
                    ]
    out[...] = spread[...].astype(BF)


def per_device(latent, w_first, w_second, w_third):
    frames, height, breadth, width = latent.shape
    mid, fine = w_first.shape[-1], w_second.shape[-1]
    last = w_third.shape[-1]
    sections = lax.axis_size("section")
    pieces, left, by = [], EARLIER, 1
    while left > 0:
        pieces.insert(0, (min(left, frames), by))
        left, by = left - frames, by + 1
    (first_of_all,) = call(lead, [((8, LANES), F32)], [], flops=COVER)
    part = [take for take, _ in pieces if take < frames]
    ends = []
    if part:
        ends = list(call(
            tails, [((take, height, breadth, width), BF) for take in part],
            [latent, first_of_all],
        ))
    got = []
    for take, by in pieces:
        ring = [(i, (i + by) % sections) for i in range(sections)]
        got.append(lax.ppermute(ends.pop(0) if take < frames else latent, "section", ring))

    rounds, cols = len(swaps(lax.axis_size("row"))), len(swaps(lax.axis_size("col")))
    total, tall = frames + EARLIER, height + 2 * RIM
    early = total - 2
    sends = call(own_rows, [((frames, RIM, breadth, width), BF)] * rounds, [latent, first_of_all])
    own_got = exchange(sends, "row")
    summed, paired, ready = call(
        kernels,
        [((3, 2, 2, mid, 4 * fine), BF), ((3, 3, 2, 2 * fine, 2 * last), BF), ((8, LANES), F32)],
        [w_second, w_third], flops=COVER,
    )

    def inner(fields, begin, count, *after):
        return call(
            functools.partial(first_inner, sources=len(fields), rows=rounds, begin=begin),
            [((count, tall - 2, breadth, mid), F32)],
            [a for field, rim in fields for a in (field, *rim)] + [w_first, *after],
            [((3, count + 2, tall, breadth, width), BF)],
            flops=2 * 27 * count * (tall - 2) * breadth * width * mid,
        )

    inners = inner([(latent, own_got)], 0, frames - 2, ready)
    earlier, *sends = call(
        functools.partial(join_frames, pieces=pieces),
        [((EARLIER, height, breadth, width), BF)] + [((EARLIER, RIM, breadth, width), BF)] * rounds,
        [inners[0], *got],
    )
    early_got = exchange(sends, "row")
    strip = ((2 * RIM, height * total, width), BF)
    scratch = [(blocked(total * height * breadth, width), F32), ((height * total, width), F32)]
    *sends, own = call(
        send_columns, [((RIM, height * total, width), BF)] * cols + [strip], [earlier, latent],
        scratch,
    )
    came = column_exchange(sends, sections)
    fields = [(earlier, early_got), (latent, own_got)]
    rest = early - (frames - 2)
    cut = rest - 1
    first_part = inner(fields, 0, cut, *sends)
    (rim,) = call(
        functools.partial(rim_columns, rows=rounds), [strip], [*early_got, *own_got, *first_part],
        scratch,
    )
    side, *sends = call(
        functools.partial(turn_columns, cols=cols, frames=total),
        [strip] + [((2 * RIM, RIM * total, width), BF)] * rounds, [*came, rim],
        [((height * total, width), F32)],
    )
    turned = exchange(sends, "row")
    inners = first_part + inner(fields, cut, rest - cut, side) + inners
    size = (tall - 2) * early
    near, far = call(
        functools.partial(first_outer, parts=len(inners), rounds=rounds),
        [((2, tall - 2, early, breadth, mid), BF), ((2, size + 8, mid), F32)],
        [*inners, own, rim, side, *turned, w_first],
        [
            ((4 * RIM, tall * total, width), F32), ((4 * RIM, 3, tall * early, width), BF),
            (blocked(size * (breadth + SLACK), mid), F32),
        ],
        flops=10**9,
    )
    later, corners = early - 2, tall - 3
    (second,) = call(
        second_conv, [((2, 2 * corners, later, breadth, 2 * fine), BF)], [near, far, summed],
        [(blocked(corners * early * (breadth + SLACK), 4 * fine), F32)],
        flops=2 * 10**9,
    )
    (out,) = call(
        third_conv, [((frames, 2 * height, 2 * breadth, last), BF)], [second, paired],
        [((frames, 2 * height, 2 * breadth, last), F32)], flops=10**9,
    )
    return out


def solution(mesh):
    in_specs = (P("section", "row", "col", None), P(), P(), P())
    out_specs = P("section", "row", "col", None)

    return jax.shard_map(
        per_device, mesh=mesh, in_specs=in_specs, out_specs=out_specs, check_vma=False
    )
```

```python
import functools

import jax
import jax.numpy as jnp
from jax import lax
from jax.experimental import pallas as pl
from jax.experimental.pallas import tpu as pltpu
from jax.sharding import PartitionSpec as P


BF, F32 = jnp.bfloat16, jnp.float32
EARLIER = 6
RIM = 2


def call(body, outs, args, scratch=(), flops=0):
    spec = pl.BlockSpec(memory_space=pltpu.VMEM)
    outs = [jax.ShapeDtypeStruct(shape, kind) for shape, kind in outs]
    size = sum(a.size * a.dtype.itemsize for a in [*args, *outs])
    return pl.pallas_call(
        body, out_shape=outs, in_specs=[spec] * len(args), out_specs=[spec] * len(outs),
        scratch_shapes=[pltpu.VMEM(*s) for s in scratch],
        cost_estimate=pl.CostEstimate(flops=flops, bytes_accessed=size, transcendentals=0),
        compiler_params=pltpu.CompilerParams(vmem_limit_bytes=32 << 20),
    )(*args)


LANES = 128
COVER = 4 * 10**9
SLACK = 8


def put(ref, rows, value):
    for k in range(ref.shape[0]):
        ref[k, rows, :] = value[:, k * LANES : (k + 1) * LANES]


def take(ref, rows, blocks=None):
    blocks = range(ref.shape[0]) if blocks is None else blocks
    return jnp.concatenate([ref[k, rows, :] for k in blocks], 1)


def blocked(rows, width):
    return (width // LANES, rows, LANES)


def swaps(size):
    assert size % 2 == 0
    rounds = [[(i, i + 1) for i in range(0, size, 2)]]
    if size > 2:
        rounds.append([(i, (i + 1) % size) for i in range(1, size, 2)])
    return [pairs + [(j, i) for i, j in pairs] for pairs in rounds]


def exchange(sends, axis):
    return [lax.ppermute(s, axis, pairs) for s, pairs in zip(sends, swaps(lax.axis_size(axis)))]


def column_exchange(sends, sections):
    rows, cols = lax.axis_size("row"), lax.axis_size("col")
    got = []
    for send, pairing in zip(sends, swaps(cols)):
        pairs = []
        for group in range(sections * rows):
            for i, j in pairing:
                to = (group ^ 1, i) if abs(i - j) > 1 else (group, j)
                pairs.append((group * cols + i, to[0] * cols + to[1]))
        got.append(lax.ppermute(send, ("section", "row", "col"), pairs))
    return got


def arrived(axis, got):
    place, size = lax.axis_index(axis), lax.axis_size(axis)
    even = place % 2 == 0
    if len(got) == 1:
        before = after = got[0]
    else:
        before, after = jnp.where(even, got[1], got[0]), jnp.where(even, got[0], got[1])
    zero = jnp.zeros_like(before)
    return jnp.where(place > 0, before, zero), jnp.where(place < size - 1, after, zero)


def lead(out):
    out[...] = jnp.zeros_like(out)


def tails(latent, lead, *outs):
    for out in outs:
        out[...] = latent[latent.shape[0] - out.shape[0] :]


def send_rows(field, sends):
    even = lax.axis_index("row") % 2 == 0
    last = field.shape[1] - RIM
    for k, send in enumerate(sends):
        start = jnp.where(even, 0, last) if k else jnp.where(even, last, 0)
        send[...] = field[:, pl.ds(start, RIM)]


def own_rows(latent, lead, *sends):
    send_rows(latent, sends)


def join_frames(*refs, pieces):
    got = refs[1 : 1 + len(pieces)]
    field, sends = refs[1 + len(pieces)], refs[2 + len(pieces) :]
    place, at = lax.axis_index("section"), 0
    for (take, by), ref in zip(pieces, got):
        field[at : at + take] = jnp.where(place >= by, ref[...], jnp.zeros_like(ref))
        at += take
    send_rows(field, sends)


def strips(fields, out, wide, narrow):
    tall, breadth, width = fields[0].shape[1:]
    size, at = tall * breadth, 0
    for field in fields:
        for t in range(field.shape[0]):
            put(wide, slice(at, at + size), field[t].astype(F32).reshape(size, width))
            at += size
    frames = at // size
    for i, c in enumerate([0, 1, breadth - 2, breadth - 1]):
        for r in range(tall):
            narrow[r * frames : (r + 1) * frames] = take(
                wide, pl.ds(r * breadth + c, frames, stride=size)
            )
        out[i] = narrow[...].astype(BF)


def send_columns(before, latent, *refs):
    sends, own, wide, narrow = refs[:-3], refs[-3], refs[-2], refs[-1]
    strips([before, latent], own, wide, narrow)
    right = lax.axis_index("col") % 2 == 0
    for k, send in enumerate(sends):
        start = jnp.where(right, 0, RIM) if k else jnp.where(right, RIM, 0)
        send[...] = own[pl.ds(start, RIM)]


def join_and_send(*refs, pieces, rounds):
    count = 1 + len(pieces)
    latent, rest = refs[count], refs[count + 1 :]
    join_frames(*refs[:count], *rest[: 1 + rounds], pieces=pieces)
    send_columns(rest[0], latent, *rest[1 + rounds :])


def rim_columns(*refs, rows):
    own, wide, narrow = refs[-3:]
    fields = []
    for got in (refs[:rows], refs[rows : 2 * rows]):
        fields.append(jnp.concatenate(arrived("row", [g[...] for g in got]), 1))
    strips(fields, own, wide, narrow)


def turn_columns(*refs, cols, frames):
    got, side, sends, narrow = refs[:cols], refs[cols + 1], refs[cols + 2 : -1], refs[-1]
    before, after = arrived("col", [g[...] for g in got])
    even = lax.axis_index("row") % 2 == 0
    size = RIM * frames
    for i, strip in enumerate([before[0], before[1], after[0], after[1]]):
        side[i] = strip
        narrow[...] = strip.astype(F32)
        first, last = narrow[:size], narrow[narrow.shape[0] - size :]
        for k, send in enumerate(sends):
            value = jnp.where(even, first, last) if k else jnp.where(even, last, first)
            send[i] = value.astype(BF)


def first_inner(*refs, sources, rows, begin):
    out, wide = refs[-2:]
    kernel = refs[sources * (1 + rows)]
    count = out.shape[0]
    frames = []
    for k in range(sources):
        field, *got = refs[k * (1 + rows) : (k + 1) * (1 + rows)]
        before, after = arrived("row", [g[...] for g in got])
        frames += [(before, field, after, t) for t in range(field.shape[0])]
    height, breadth, width = frames[0][1].shape[1:]
    tall = height + 2 * RIM
    size = tall * breadth
    col = lax.broadcasted_iota(jnp.int32, (size, width), 0) % breadth
    for t in range(count + 2):
        *parts, at = frames[begin + t]
        rows_of = jnp.concatenate([part[at] for part in parts], 0)
        wide[1, t] = rows_of
        flat = rows_of.reshape(size, width).astype(F32)
        lower = jnp.where(col == 0, 0.0, pltpu.roll(flat, 1, 0))
        upper = jnp.where(col == breadth - 1, 0.0, pltpu.roll(flat, size - 1, 0))
        wide[0, t] = lower.astype(BF).reshape(rows_of.shape)
        wide[2, t] = upper.astype(BF).reshape(rows_of.shape)
    taps = [
        wide[e, a : a + count, b : b + tall - 2].reshape(-1, width)
        for a in range(3) for b in range(3) for e in range(3)
    ]
    found = jnp.dot(
        jnp.concatenate(taps, 1), kernel[...].reshape(-1, kernel.shape[-1]), preferred_element_type=F32
    )
    out[...] = found.reshape(out.shape)


def kernels(second, third, summed, paired, ready):
    ready[...] = jnp.zeros_like(ready)
    fine = second.shape[-1]
    reads = [[(0, 1), (2,)], [(0,), (1, 2)]]
    for a in range(3):
        tap = [[second[a, b, e].astype(F32) for e in range(3)] for b in range(3)]
        for di in range(2):
            for dj in range(2):
                for py in range(2):
                    for px in range(2):
                        parts = [tap[b][e] for b in reads[py][di] for e in reads[px][dj]]
                        at = (2 * py + px) * fine
                        summed[a, di, dj, :, at : at + fine] = sum(parts[1:], parts[0]).astype(BF)
    width, out = third.shape[-2:]
    for a in range(3):
        for b in range(3):
            for dj in range(2):
                for px in range(2):
                    for q in range(2):
                        e = 2 * dj + px - q
                        block = third[a, b, e] if 0 <= e < 3 else jnp.zeros((width, out), BF)
                        paired[a, b, dj, px * width : (px + 1) * width, q * out : (q + 1) * out] = block


def limits(axis):
    return lax.axis_index(axis) == 0, lax.axis_index(axis) == lax.axis_size(axis) - 1


def first_outer(*refs, parts, rounds):
    inner, own, rim, side = refs[:parts], *refs[parts : parts + 3]
    turned = refs[parts + 3 : parts + 3 + rounds]
    kernel, near, far, edge, moved, coarse = refs[parts + 3 + rounds :]
    rows, breadth, width = inner[0].shape[1:]
    frames = sum(part.shape[0] for part in inner)
    total, tall = frames + 2, rows + 2
    (top, bottom), (leftmost, rightmost) = limits("row"), limits("col")

    above, below = arrived("row", [g[...] for g in turned])
    ends = RIM * total
    full = tall * total
    for i in range(RIM):
        for k, (main, at) in enumerate([(side, i), (own, i), (own, RIM + i), (side, RIM + i)]):
            strip = edge.at[k * RIM + i]
            strip[ends : full - ends] = main[at].astype(F32)
            if main is own:
                strip[:ends] = rim[at, :ends].astype(F32)
                strip[full - ends : full] = rim[at, ends : 2 * ends].astype(F32)
            else:
                strip[:ends] = above[at].astype(F32)
                strip[full - ends : full] = below[at].astype(F32)
    for i in range(4 * RIM):
        for a in range(3):
            moved[i, a] = jnp.concatenate(
                [edge[i, r * total + a : r * total + a + frames] for r in range(tall)], 0
            ).astype(BF)
    size = rows * frames
    lhs = jnp.concatenate([
        jnp.concatenate(
            [moved[i + e, a, b * frames : b * frames + size] for i in (0, 1, 4, 5)], 0
        )
        for a in range(3) for b in range(3) for e in range(3)
    ], 1)
    found = jnp.dot(lhs, kernel[...].reshape(-1, kernel.shape[-1]), preferred_element_type=F32)
    left, begin, end, right = [found[i * size : (i + 1) * size] for i in range(4)]

    pitch = breadth + SLACK
    count = 0
    for part in inner:
        for t in range(part.shape[0]):
            for r in range(rows):
                at = (r * frames + count) * pitch
                put(coarse, slice(at, at + breadth), part[t, r])
            count += 1
    put(coarse, pl.ds(0, size, stride=pitch), begin)
    put(coarse, pl.ds(breadth - 1, size, stride=pitch), end)
    put(coarse, pl.ds(breadth, size, stride=pitch), right)

    slot = lax.broadcasted_iota(jnp.int32, (breadth, width), 0)
    ends = rightmost & (slot == breadth - 1)
    for r in range(rows):
        lost = top if r == 0 else bottom if r == rows - 1 else None
        for t in range(frames):
            at = (r * frames + t) * pitch
            for dj in range(2):
                value = jnp.maximum(take(coarse, slice(at + dj, at + dj + breadth)), 0.0)
                gone = [g for g in (lost, ends if dj else None) if g is not None]
                if gone:
                    value = jnp.where(functools.reduce(jnp.logical_or, gone), 0.0, value)
                near[dj, r, t] = value.astype(BF)
    row = lax.broadcasted_iota(jnp.int32, (size, width), 0) // frames
    outside = (top & (row == 0)) | (bottom & (row == rows - 1))
    far[0, :size] = jnp.where(outside | leftmost, 0.0, jnp.maximum(left, 0.0))
    far[1, :size] = jnp.where(outside, 0.0, jnp.maximum(begin, 0.0))


def second_conv(near, far, summed, fine, grown):
    _, rows, frames, breadth, width = near.shape
    pitch = breadth + SLACK
    (top, bottom), (leftmost, rightmost) = limits("row"), limits("col")
    corners, later = rows - 1, frames - 2
    short = corners * frames
    taps = [
        jnp.concatenate([
            near[dj, di : di + corners, a : a + later].reshape(-1, width),
            far[dj, di * frames + a : di * frames + a + short].astype(BF),
        ], 0)
        for a in range(3) for di in range(2) for dj in range(2)
    ]
    found = jnp.dot(
        jnp.concatenate(taps, 1), summed[...].reshape(-1, summed.shape[-1]), preferred_element_type=F32
    )
    found = jnp.maximum(found, 0.0)
    full = later * corners * breadth
    half = found.shape[1] // 2
    for i in range(corners):
        for t in range(later):
            at, to = (i * later + t) * breadth, (i * frames + t) * pitch + SLACK
            put(grown, slice(to, to + breadth), found[at : at + breadth])
    put(grown, pl.ds(SLACK - 1, short, stride=pitch), found[full:])
    slot = lax.broadcasted_iota(jnp.int32, (breadth, half), 0)
    side = lax.broadcasted_iota(jnp.int32, (breadth, half), 1) < half // 2
    begins = leftmost & (slot == 0) & side
    ends = rightmost & (slot == breadth - 1) & ~side
    for t in range(later):
        for i in range(corners):
            for py in range(2):
                blocks = range(py * half // LANES, (py + 1) * half // LANES)
                lost = (top if py == 0 and i == 0 else bottom if py == 1 and i == corners - 1 else None)
                for dj, gone in enumerate((begins, ends)):
                    gone = gone if lost is None else gone | lost
                    at = (i * frames + t) * pitch + SLACK - 1 + dj
                    value = take(grown, slice(at, at + breadth), blocks)
                    fine[dj, 2 * i + py, t] = jnp.where(gone, 0.0, value).astype(BF)


def third_conv(fine, paired, out, spread):
    _, high, later, breadth, half = fine.shape
    high, kept, wide = high - 2, later - 2, out.shape[-1]
    kernel = paired[...].reshape(-1, paired.shape[-1])
    step = high // 2
    for begin in range(0, high, step):
        taps = [
            fine[dj, begin + b : begin + b + step, a : a + kept].reshape(-1, half)
            for a in range(3) for b in range(3) for dj in range(2)
        ]
        found = jnp.dot(jnp.concatenate(taps, 1), kernel, preferred_element_type=F32)
        for y in range(step):
            for t in range(kept):
                at = (y * kept + t) * breadth
                for q in range(2):
                    spread[t, begin + y, pl.ds(q, breadth, stride=2), :] = found[
                        at : at + breadth, q * wide : (q + 1) * wide
                    ]
    out[...] = spread[...].astype(BF)


def per_device(latent, w_first, w_second, w_third):
    frames, height, breadth, width = latent.shape
    mid, fine = w_first.shape[-1], w_second.shape[-1]
    last = w_third.shape[-1]
    sections = lax.axis_size("section")
    pieces, left, by = [], EARLIER, 1
    while left > 0:
        pieces.insert(0, (min(left, frames), by))
        left, by = left - frames, by + 1
    (first_of_all,) = call(lead, [((8, LANES), F32)], [], flops=COVER)
    part = [take for take, _ in pieces if take < frames]
    ends = []
    if part:
        ends = list(call(
            tails, [((take, height, breadth, width), BF) for take in part],
            [latent, first_of_all],
        ))
    got = []
    for take, by in pieces:
        ring = [(i, (i + by) % sections) for i in range(sections)]
        got.append(lax.ppermute(ends.pop(0) if take < frames else latent, "section", ring))

    rounds, cols = len(swaps(lax.axis_size("row"))), len(swaps(lax.axis_size("col")))
    total, tall = frames + EARLIER, height + 2 * RIM
    early = total - 2
    sends = call(own_rows, [((frames, RIM, breadth, width), BF)] * rounds, [latent, first_of_all])
    own_got = exchange(sends, "row")
    summed, paired, ready = call(
        kernels,
        [((3, 2, 2, mid, 4 * fine), BF), ((3, 3, 2, 2 * fine, 2 * last), BF), ((8, LANES), F32)],
        [w_second, w_third], flops=COVER,
    )

    def inner(fields, begin, count, *after):
        return call(
            functools.partial(first_inner, sources=len(fields), rows=rounds, begin=begin),
            [((count, tall - 2, breadth, mid), F32)],
            [a for field, rim in fields for a in (field, *rim)] + [w_first, *after],
            [((3, count + 2, tall, breadth, width), BF)],
            flops=2 * 27 * count * (tall - 2) * breadth * width * mid,
        )

    inners = inner([(latent, own_got)], 0, frames - 2, ready)
    strip = ((2 * RIM, height * total, width), BF)
    scratch = [(blocked(total * height * breadth, width), F32), ((height * total, width), F32)]
    earlier, *sends, own = call(
        functools.partial(join_and_send, pieces=pieces, rounds=rounds),
        [((EARLIER, height, breadth, width), BF)] + [((EARLIER, RIM, breadth, width), BF)] * rounds
        + [((RIM, height * total, width), BF)] * cols + [strip],
        [inners[0], *got, latent], scratch,
    )
    early_got = exchange(sends[:rounds], "row")
    sends = sends[rounds:]
    came = column_exchange(sends, sections)
    fields = [(earlier, early_got), (latent, own_got)]
    rest = early - (frames - 2)
    cut = 2 * rest // 3
    first_part = inner(fields, 0, cut, *sends)
    (rim,) = call(
        functools.partial(rim_columns, rows=rounds), [strip], [*early_got, *own_got, *first_part],
        scratch,
    )
    side, *sends = call(
        functools.partial(turn_columns, cols=cols, frames=total),
        [strip] + [((2 * RIM, RIM * total, width), BF)] * rounds, [*came, rim],
        [((height * total, width), F32)],
    )
    turned = exchange(sends, "row")
    inners = first_part + inner(fields, cut, rest - cut, side) + inners
    size = (tall - 2) * early
    near, far = call(
        functools.partial(first_outer, parts=len(inners), rounds=rounds),
        [((2, tall - 2, early, breadth, mid), BF), ((2, size + 8, mid), F32)],
        [*inners, own, rim, side, *turned, w_first],
        [
            ((4 * RIM, tall * total, width), F32), ((4 * RIM, 3, tall * early, width), BF),
            (blocked(size * (breadth + SLACK), mid), F32),
        ],
        flops=10**9,
    )
    later, corners = early - 2, tall - 3
    (second,) = call(
        second_conv, [((2, 2 * corners, later, breadth, 2 * fine), BF)], [near, far, summed],
        [(blocked(corners * early * (breadth + SLACK), 4 * fine), F32)],
        flops=2 * 10**9,
    )
    (out,) = call(
        third_conv, [((frames, 2 * height, 2 * breadth, last), BF)], [second, paired],
        [((frames, 2 * height, 2 * breadth, last), F32)], flops=10**9,
    )
    return out


def solution(mesh):
    in_specs = (P("section", "row", "col", None), P(), P(), P())
    out_specs = P("section", "row", "col", None)

    return jax.shard_map(
        per_device, mesh=mesh, in_specs=in_specs, out_specs=out_specs, check_vma=False
    )
```
